32 devices in a mesh: past: 2 (over y), second: 16 (over z, x, core).
Axes of the slice: x: 2, y: 2, z: 4, core: 2. Of those that a mesh axis runs over, the one named last changes fastest.
Arguments:
- green_row: float32 [256, 64, 128], P('second'), may hold values from -4 to 4
- green_hist: float32 [8, 256, 64, 128], P('past', 'second'), may hold values from -5.25 to 5.25, as said below
- hamiltonian: float32 [64, 128], replicated, may hold values from -0.75 to 0.75
- quad_table: float32 [8], replicated, may hold values from 0.2 to 2
- weight_index: int32 [8], P('past'), may hold values from 0 to 7
- block_start: int32 [1], replicated, may hold values from 0 to 248
Outputs:
- green_next: float32 [256, 64, 128], P('second')
- change_norm: float32 [1], replicated
The draws below stay inside these ranges and needn't reach their ends.
Inputs may be any that keep to these rules, and one draw needn't show every extreme that they name: `green_hist`: real numbers of order one; magnitudes differ between second times.
All inputs are finite; a program needn't handle non-finite values.
Results may differ from the reference program's by a relative error of at most 0.0003.
Values sent between devices are 32-bit elements; how exact they have to be, the bound alone decides.
No kernel may reach another device: no remote copies, remote signals or barrier semaphores. Data moves between devices by JAX's collectives and lax.ppermute only.
A program may use at most 64 MiB of HBM per device.

```python
import math
import jax
import jax.numpy as jnp
from jax import lax

NO = 64
SEC_DEV = 16
NQ = 8
PT = 8
NS = 256
N_SECOND = 16


def draw_green_hist(key, part):
    scale_key = jax.random.fold_in(key, 11)
    value_key = jax.random.fold_in(key, 23)
    rough = jnp.exp(jax.random.uniform(scale_key, (NS,), jnp.float32, math.log(0.3), math.log(1.5)))
    rising = 3.0 ** (jnp.arange(NS, dtype=jnp.float32) / NS - 1.0)
    column_scale = (rough * rising)[None, :, None, None]
    values = jnp.clip(jax.random.normal(value_key, (PT, NS, NO, 2 * NO), jnp.float32), -3.5, 3.5)
    return (values * column_scale).astype(jnp.float32)


def set_ends(entries, key, smallest, top_value):
    extent = entries.shape
    place = [jax.random.randint(jax.random.fold_in(key, axis), (), 0, extent[axis]) for axis in range(len(extent))]
    entries = entries.at[tuple(place)].set(smallest)
    longest = extent.index(max(extent))
    place[longest] = (place[longest] + 1) % extent[longest]
    return entries.at[tuple(place)].set(top_value)


def block_scale(rng, dims, pieces, smallest, high):
    def one(dim, blocks):
        steps = jax.random.uniform(jax.random.fold_in(jax.random.fold_in(rng, 6), dim), (blocks,), jnp.float32, smallest / len(pieces), high / len(pieces))
        return jnp.repeat(jnp.exp(steps), dims[dim] // blocks).reshape((-1,) + (1,) * (len(dims) - dim - 1))

    loudness = one(*pieces[0])
    for cut in pieces[1:]:
        loudness = loudness * one(*cut)
    return loudness


def noise(own_key, extent, scale, most, pieces=(), kind=jnp.bfloat16):
    array = jax.random.normal(own_key, extent, jnp.float32) * scale
    if len(pieces) > 0:
        array = block_scale(own_key, extent, pieces, -0.22, 0.18) * array
    return jnp.clip(array, min=-most, max=most).astype(kind)


def setup_inputs(seed: int = 0) -> dict:
    streams_of = jax.random.split(jax.random.key(seed), 7)
    return {
        "green_row": noise(streams_of[0], (NS, NO, 2 * NO), 0.7, 4.0, ((0, 16),), jnp.float32),
        "green_hist": draw_green_hist(jax.random.fold_in(streams_of[6], 71), 0),
        "hamiltonian": noise(streams_of[2], (NO, 2 * NO), NO ** -0.5, 0.75, (), jnp.float32),
        "quad_table": jnp.clip(jnp.exp(jax.random.uniform(streams_of[3], (NQ,), jnp.float32, math.log(0.2), math.log(2.0))), 0.2, 2.0),
        "weight_index": set_ends(jax.random.randint(streams_of[4], (PT,), 0, NQ), jax.random.fold_in(streams_of[4], 1), 0, NQ - 1).astype(jnp.int32),
        "block_start": jax.random.randint(streams_of[5], (1,), 0, NS - PT + 1).astype(jnp.int32),
    }


coupling = 0.5
step_size = 0.25

def rotate(tiles):
    return jnp.concatenate([-tiles[..., NO:], tiles[..., :NO]], axis=-1)

def self_energy(tiles):
    magnitude = tiles[..., :NO] ** 2 + tiles[..., NO:] ** 2
    return -coupling * jnp.concatenate([magnitude, magnitude], axis=-1) * tiles

def apply_ham(herm_real, herm_imag, tiles):
    first = jnp.einsum('ij,sjk->sik', herm_real, tiles, precision=lax.Precision.HIGHEST)
    second = jnp.einsum('ij,sjk->sik', herm_imag, rotate(tiles), precision=lax.Precision.HIGHEST)
    return first + second

def memory(tiles_in, green_hist, weights, window_start):
    window = lax.dynamic_slice_in_dim(tiles_in, window_start, PT, 0)
    weight_col = weights[:, None, None]
    left_side = jnp.stack([weight_col * self_energy(window), weight_col * window])
    left_side = jnp.stack([left_side[..., :NO], left_side[..., NO:]])
    norm_scale = 1.0 / math.sqrt(NO * PT)

    def block(block_index):
        hist_block = lax.dynamic_slice_in_dim(green_hist, (block_index * SEC_DEV).astype(jnp.int32), SEC_DEV, 1)
        right_side = jnp.stack([hist_block, self_energy(hist_block)])
        contracted = jnp.einsum('cqpij,qpsjk->csik', left_side, right_side, precision=lax.Precision.HIGHEST)
        return norm_scale * (contracted[0] + rotate(contracted[1]))
    blocks = lax.map(block, jnp.arange(N_SECOND, dtype=jnp.int32))
    return blocks.reshape(NS, NO, 2 * NO)

def reference(green_row, green_hist, hamiltonian, quad_table, weight_index, block_start):
    ham_real = hamiltonian[:, :NO]
    ham_imag = hamiltonian[:, NO:]
    herm_real = 0.5 * (ham_real + ham_real.T)
    herm_imag = 0.5 * (ham_imag - ham_imag.T)
    weights = jnp.take(quad_table, weight_index, axis=0)
    window_start = block_start[0].astype(jnp.int32)

    def derive(tiles_in):
        combined = apply_ham(herm_real, herm_imag, tiles_in) + memory(tiles_in, green_hist, weights, window_start)
        return jnp.concatenate([combined[..., NO:], -combined[..., :NO]], axis=-1)
    slope_one = derive(green_row)
    predicted = green_row + step_size * slope_one
    slope_two = derive(predicted)
    green_next = green_row + 0.5 * step_size * (slope_one + slope_two)
    square_sum = jnp.sum((green_next - predicted) ** 2)
    change = jnp.sqrt(square_sum / (NS * NO * 2 * NO)) / step_size
    return (green_next, change.reshape(1))
```

```python
import math

import jax
import jax.numpy as jnp
from jax import lax
from jax.experimental import pallas as pl
from jax.experimental.pallas import tpu as pltpu
from jax.sharding import PartitionSpec as P

coupling = 0.5
step_size = 0.25

f32 = jnp.float32
bf16 = jnp.bfloat16
SMEM_SPEC = pl.BlockSpec(memory_space=pltpu.SMEM)
VMEM_SPEC = pl.BlockSpec(memory_space=pltpu.VMEM)


def split(value):
    high = value.astype(bf16)
    return high, (value - high.astype(f32)).astype(bf16)


def dot3(left, right):
    def one(a, b):
        return jnp.dot(a, b, preferred_element_type=f32)

    return one(left[0], right[0]) + (one(left[0], right[1]) + one(left[1], right[0]))


def swap_halves(tile):
    return pltpu.roll(tile, tile.shape[-1] // 2, tile.ndim - 1)


def is_real(shape):
    return lax.broadcasted_iota(jnp.int32, shape, len(shape) - 1) < shape[-1] // 2


def self_energy(tile):
    square = tile * tile
    return -coupling * (square + swap_halves(square)) * tile


def minus_i_times(acc, orbits):
    turned = swap_halves(acc[:orbits])
    return acc[orbits:] + jnp.where(is_real(turned.shape), turned, -turned)


def left_factor(tile, weight):
    scaled = weight * self_energy(tile)
    plain = weight * tile
    real = is_real(tile.shape)
    return jnp.concatenate(
        [jnp.where(real, scaled, swap_halves(plain)), jnp.where(real, swap_halves(scaled), plain)], axis=0
    )


def right_factor(tiles):
    return jnp.concatenate(
        [jnp.concatenate(tiles, axis=1), jnp.concatenate([self_energy(t) for t in tiles], axis=1)], axis=0
    )


def prepare_kernel(pos_ref, inside_ref, row_ref, ham_ref, window_ref, herm_ref):
    count = window_ref.shape[0]
    orbits = ham_ref.shape[0]
    for p in range(count):
        window_ref[p] = jnp.where(inside_ref[p] > 0, row_ref[pos_ref[p]], 0.0)
    real = ham_ref[:, :orbits]
    imag = ham_ref[:, orbits:]
    herm_ref[...] = jnp.concatenate([0.5 * (real + real.T), 0.5 * (imag - imag.T)], axis=0)


def prepare(pos, inside, green_row, hamiltonian):
    count = pos.shape[0]
    orbits = hamiltonian.shape[0]
    return pl.pallas_call(
        prepare_kernel,
        in_specs=[SMEM_SPEC, SMEM_SPEC, VMEM_SPEC, VMEM_SPEC],
        out_specs=[VMEM_SPEC, VMEM_SPEC],
        out_shape=[
            jax.ShapeDtypeStruct((count,) + green_row.shape[1:], f32),
            jax.ShapeDtypeStruct((2 * orbits, orbits), f32),
        ],
        name="prepare",
    )(pos, inside, green_row, hamiltonian)


def owner_kernel(
    pos_ref, inside_ref, quad_ref, index_ref, own_ref, win_ref, base_ref, herm_ref, hist_a, hist_b, out_ref, hi, lo,
    *, scale
):
    past_rows, orbits, width = win_ref.shape
    step = pl.program_id(0)

    @pl.when(step == 0)
    def _():
        for p in range(past_rows):
            high, low = split(left_factor(win_ref[p], quad_ref[index_ref[p]]))
            hi[:, p * width : (p + 1) * width] = high
            lo[:, p * width : (p + 1) * width] = low

    right = jnp.concatenate([right_factor([hist_a[p, 0], hist_b[p, 0]]) for p in range(past_rows)], axis=0)
    acc = dot3((hi[...], lo[...]), split(right))
    part = step_size * scale * jnp.concatenate(
        [minus_i_times(acc[:, :width], orbits)[None], minus_i_times(acc[:, width:], orbits)[None]], axis=0
    )
    for q in range(2):
        out_ref[q] = jnp.where(inside_ref[2 * step + q] > 0, part[q], 0.0)

    first = own_ref[0]

    @pl.when((2 * step >= first) & (2 * step < first + past_rows))
    def _():
        base = jnp.concatenate([base_ref[2 * step - first], base_ref[2 * step + 1 - first]], axis=1)
        acc_ham = dot3(split(herm_ref[...]), split(base))
        for q in range(2):
            cols = slice(q * width, (q + 1) * width)
            out_ref[q] += base[:, cols] + step_size * minus_i_times(acc_ham[:, cols], orbits)


def owner_part(pos, inside, quad_table, weight_index, first, window, base, herm, green_hist, scale):
    past_rows, _, orbits, width = green_hist.shape
    total = pos.shape[0]
    fixed = lambda shape: pl.BlockSpec(shape, lambda i, *_: (0,) * len(shape))
    return pl.pallas_call(
        lambda *refs: owner_kernel(*refs, scale=scale),
        grid_spec=pltpu.PrefetchScalarGridSpec(
            num_scalar_prefetch=5,
            grid=(total // 2,),
            in_specs=[
                fixed(window.shape),
                fixed(base.shape),
                fixed(herm.shape),
                pl.BlockSpec((past_rows, 1, orbits, width), lambda i, pos, *_: (0, pos[2 * i], 0, 0)),
                pl.BlockSpec((past_rows, 1, orbits, width), lambda i, pos, *_: (0, pos[2 * i + 1], 0, 0)),
            ],
            out_specs=pl.BlockSpec((2, orbits, width), lambda i, *_: (i, 0, 0)),
            scratch_shapes=[pltpu.VMEM((2 * orbits, past_rows * width), bf16)] * 2,
        ),
        out_shape=jax.ShapeDtypeStruct((total, orbits, width), f32),
        name="owner_part",
    )(pos, inside, quad_table, weight_index, first, window, base, herm, green_hist, green_hist)


def integral_kernel(quad_ref, index_ref, odd_ref, mine_ref, other_ref, hist_ref, out_ref, hi, lo, *, scale):
    past_rows, group, orbits, width = hist_ref.shape
    half = past_rows // 2

    @pl.when(pl.program_id(0) == 0)
    def _():
        for p in range(past_rows):
            here = odd_ref[0] == p // half
            tile = jnp.where(here, mine_ref[p % half], other_ref[p % half])
            high, low = split(left_factor(tile, quad_ref[index_ref[p]]))
            hi[:, p * width : (p + 1) * width] = high
            lo[:, p * width : (p + 1) * width] = low

    for s in range(0, group, 2):
        right = jnp.concatenate(
            [right_factor([hist_ref[p, s], hist_ref[p, s + 1]]) for p in range(past_rows)], axis=0
        )
        acc = dot3((hi[...], lo[...]), split(right))
        for q in range(2):
            out_ref[s + q] = scale * minus_i_times(acc[:, q * width : (q + 1) * width], orbits)


def integral(quad_table, weight_index, odd, mine, other, green_hist, scale, name):
    past_rows, sec_rows, orbits, width = green_hist.shape
    group = 4
    fixed = lambda shape: pl.BlockSpec(shape, lambda i: (0,) * len(shape))
    return pl.pallas_call(
        lambda *refs: integral_kernel(*refs, scale=scale),
        grid=(sec_rows // group,),
        in_specs=[
            SMEM_SPEC,
            SMEM_SPEC,
            SMEM_SPEC,
            fixed(mine.shape),
            fixed(other.shape),
            pl.BlockSpec((past_rows, group, orbits, width), lambda i: (0, i, 0, 0)),
        ],
        out_specs=pl.BlockSpec((group, orbits, width), lambda i: (i, 0, 0)),
        scratch_shapes=[pltpu.VMEM((2 * orbits, past_rows * width), bf16)] * 2,
        out_shape=jax.ShapeDtypeStruct((sec_rows, orbits, width), f32),
        name=name,
    )(quad_table, weight_index, odd, mine, other, green_hist)


def share_kernel(row_ref, sum_ref, herm_ref, out_base_ref, diff_base_ref):
    share, orbits, width = row_ref.shape
    herm = split(herm_ref[...])
    for s in range(0, share, 2):
        def pair(ref):
            return jnp.concatenate([ref[s], ref[s + 1]], axis=1)

        def ham(value):
            acc = dot3(herm, split(value))
            return jnp.concatenate(
                [minus_i_times(acc[:, q * width : (q + 1) * width], orbits) for q in range(2)], axis=1
            )

        row = pair(row_ref)
        slope = ham(row) + pair(sum_ref)
        turned = ham(row + step_size * slope)
        out_base = row + 0.5 * step_size * (slope + turned)
        diff_base = 0.5 * step_size * (turned - slope)
        for q in range(2):
            cols = slice(q * width, (q + 1) * width)
            out_base_ref[s + q] = out_base[:, cols]
            diff_base_ref[s + q] = diff_base[:, cols]


def share_bases(row, slope_sum, herm):
    shape = jax.ShapeDtypeStruct(row.shape, f32)
    return pl.pallas_call(
        share_kernel,
        in_specs=[VMEM_SPEC] * 3,
        out_specs=[VMEM_SPEC] * 2,
        out_shape=[shape, shape],
        name="share_bases",
    )(row, slope_sum, herm)


def exchange(value, axis, mask):
    size = lax.axis_size(axis)
    return lax.ppermute(value, axis, [(i, i ^ mask) for i in range(size)])


def pick(value, index, axis=0):
    return lax.dynamic_index_in_dim(value, index, axis, keepdims=False)


def scatter_past(value):
    size = lax.axis_size("past")
    index = lax.axis_index("past")
    while size > 1:
        half = size // 2
        value = value.reshape((2, half) + value.shape[1:])
        upper = (index // half) % 2
        value = pick(value, upper) + exchange(pick(value, 1 - upper), "past", half)
        size = half
    return value[0]


def gather_past(value):
    size = lax.axis_size("past")
    index = lax.axis_index("past")
    value = value[None]
    mask = 1
    while mask < size:
        other = exchange(value, "past", mask)
        upper = (index // mask) % 2 == 1
        value = jnp.concatenate([jnp.where(upper, other, value), jnp.where(upper, value, other)], axis=0)
        mask *= 2
    return value


def spread_second(value):
    mask = 2
    while mask < lax.axis_size("second"):
        value = value + exchange(value, "second", mask)
        mask *= 2
    return value


def local(green_row, green_hist, hamiltonian, quad_table, weight_index, block_start):
    orbits = hamiltonian.shape[0]
    sec_rows = green_row.shape[0]
    past_rows = green_hist.shape[0]
    width = green_row.shape[-1]
    past_size = lax.axis_size("past")
    second_size = lax.axis_size("second")
    total_past = past_rows * past_size
    past_index = lax.axis_index("past")
    second_index = lax.axis_index("second")
    odd = second_index % 2
    odd_arg = odd.reshape(1)
    scale = 1.0 / math.sqrt(orbits * total_past)

    spot = block_start[0] - second_index * sec_rows + jnp.arange(total_past, dtype=jnp.int32)
    inside = ((spot >= 0) & (spot < sec_rows)).astype(jnp.int32)
    pos = jnp.clip(spot, 0, sec_rows - 1)
    first = past_index * past_rows
    own_pos = lax.dynamic_slice_in_dim(pos, first, past_rows)
    own_inside = lax.dynamic_slice_in_dim(inside, first, past_rows)
    own_window, herm = prepare(own_pos, own_inside, green_row, hamiltonian)

    halves = own_window.reshape(2, past_rows // 2, orbits, width)
    row_mine = spread_second(pick(halves, odd) + exchange(pick(halves, 1 - odd), "second", 1))
    row_other = exchange(row_mine, "second", 1)

    owner = block_start[0] // sec_rows
    crossing = (block_start[0] + total_past - 1) // sec_rows > owner
    flips = owner ^ (owner + 1)
    branch = jnp.where(crossing, 1, 0)
    masks = []
    while 2 ** len(masks) < second_size:
        masks.append(2 ** (len(masks) + 1) - 1)
    for mask in masks[:-1]:
        branch = branch + jnp.where(crossing & (flips > mask), 1, 0)
    window = lax.switch(
        branch,
        [lambda w: w] + [lambda w, mask=mask: w + exchange(w, "second", mask) for mask in masks],
        own_window,
    )
    part = owner_part(
        pos, inside, quad_table, weight_index, first.reshape(1), window, own_window, herm, green_hist, scale
    )

    parts = part.reshape(past_size, 2, past_rows // 2, orbits, width)
    parts = pick(parts, odd, 1) + exchange(pick(parts, 1 - odd, 1), "second", 1)
    pred_mine = spread_second(scatter_past(parts))
    pred_other = exchange(pred_mine, "second", 1)

    share_rows = sec_rows // past_size
    row_share = lax.dynamic_slice_in_dim(green_row, past_index * share_rows, share_rows, 0)

    def by_share(value):
        return value.reshape((past_size, share_rows) + value.shape[1:])

    slope_part = integral(quad_table, weight_index, odd_arg, row_mine, row_other, green_hist, scale, "integral_row")
    slope_sum = scatter_past(by_share(slope_part))
    out_base, diff_base = share_bases(row_share, slope_sum, herm)

    last_part = integral(
        quad_table, weight_index, odd_arg, pred_mine, pred_other, green_hist, 0.5 * step_size * scale, "integral_pred"
    )
    last_sum = scatter_past(by_share(last_part))
    out_share = out_base + last_sum
    square_sum = jnp.sum((diff_base + last_sum) ** 2)
    green_next = gather_past(out_share).reshape(green_row.shape)

    devices = past_size * second_size
    lanes = jnp.broadcast_to(square_sum.reshape(1, 1), (devices, 128))
    sums = lax.all_to_all(lanes, ("past", "second"), 0, 0, tiled=True)
    total = jnp.sum(sums[:, :1])
    entry_count = sec_rows * second_size * orbits * width
    change = jnp.sqrt(total / entry_count) / step_size
    return (green_next, change.reshape(1))


def solution(mesh):
    placed = (P("second", None, None), P("past", "second", None, None), P(), P(), P("past"), P())
    return jax.shard_map(
        local, mesh=mesh, in_specs=placed, out_specs=(P("second", None, None), P()), check_vma=False
    )
```

```python
import math

import jax
import jax.numpy as jnp
from jax import lax
from jax.experimental import pallas as pl
from jax.experimental.pallas import tpu as pltpu
from jax.sharding import PartitionSpec as P

coupling = 0.5
step_size = 0.25

f32 = jnp.float32
bf16 = jnp.bfloat16
SMEM_SPEC = pl.BlockSpec(memory_space=pltpu.SMEM)
VMEM_SPEC = pl.BlockSpec(memory_space=pltpu.VMEM)
PARAMS = pltpu.CompilerParams(vmem_limit_bytes=12 << 20)


def split(value):
    high = value.astype(bf16)
    return high, (value - high.astype(f32)).astype(bf16)


def dot3(left, right):
    def one(a, b):
        return jnp.dot(a, b, preferred_element_type=f32)

    return one(left[0], right[0]) + (one(left[0], right[1]) + one(left[1], right[0]))


def swap_halves(tile):
    return pltpu.roll(tile, tile.shape[-1] // 2, tile.ndim - 1)


def is_real(shape):
    return lax.broadcasted_iota(jnp.int32, shape, len(shape) - 1) < shape[-1] // 2


def self_energy(tile):
    square = tile * tile
    return -coupling * (square + swap_halves(square)) * tile


def minus_i_times(acc, orbits):
    turned = swap_halves(acc[:orbits])
    return acc[orbits:] + jnp.where(is_real(turned.shape), turned, -turned)


def left_factor(tile, weight):
    scaled = weight * self_energy(tile)
    plain = weight * tile
    real = is_real(tile.shape)
    return jnp.concatenate(
        [jnp.where(real, scaled, swap_halves(plain)), jnp.where(real, swap_halves(scaled), plain)], axis=0
    )


def local_spot(start_ref, tile, sec_rows):
    spot = start_ref[0] - lax.axis_index("second") * sec_rows + tile
    return jnp.clip(spot, 0, sec_rows - 1), (spot >= 0) & (spot < sec_rows)


def prepare_kernel(start_ref, row_ref, ham_ref, window_ref, keep_ref, send_ref, herm_ref):
    count = window_ref.shape[0]
    half = count // 2
    orbits = ham_ref.shape[0]
    first = lax.axis_index("past") * count
    odd = lax.axis_index("second") % 2
    for p in range(count):
        pos, inside = local_spot(start_ref, first + p, row_ref.shape[0])
        window_ref[p] = jnp.where(inside, row_ref[pos], 0.0)
    for p in range(half):
        keep_ref[p] = window_ref[odd * half + p]
        send_ref[p] = window_ref[(1 - odd) * half + p]
    real = ham_ref[:, :orbits]
    imag = ham_ref[:, orbits:]
    herm_ref[...] = jnp.concatenate([0.5 * (real + real.T), 0.5 * (imag - imag.T)], axis=0)


def prepare(block_start, green_row, hamiltonian, count):
    orbits = hamiltonian.shape[0]
    tile = green_row.shape[1:]
    half = jax.ShapeDtypeStruct((count // 2,) + tile, f32)
    return pl.pallas_call(
        prepare_kernel,
        in_specs=[SMEM_SPEC, VMEM_SPEC, VMEM_SPEC],
        out_specs=[VMEM_SPEC] * 4,
        out_shape=[
            jax.ShapeDtypeStruct((count,) + tile, f32),
            half,
            half,
            jax.ShapeDtypeStruct((2 * orbits, orbits), f32),
        ],
        compiler_params=PARAMS,
        name="prepare",
    )(block_start, green_row, hamiltonian)


def right_kernel(hist_ref, high_ref, low_ref):
    past_rows, sec_rows, orbits, _ = hist_ref.shape

    def body(s, carry):
        for p in range(past_rows):
            tile = hist_ref[p, s]
            for q, part in enumerate((tile, self_energy(tile))):
                rows = slice((2 * p + q) * orbits, (2 * p + q + 1) * orbits)
                high_ref[s, rows], low_ref[s, rows] = split(part)
        return carry

    lax.fori_loop(0, sec_rows, body, 0, unroll=2)


def right_factors(green_hist):
    past_rows, sec_rows, orbits, width = green_hist.shape
    shape = jax.ShapeDtypeStruct((sec_rows, past_rows * 2 * orbits, width), bf16)
    return pl.pallas_call(
        right_kernel,
        in_specs=[VMEM_SPEC],
        out_specs=[VMEM_SPEC] * 2,
        out_shape=[shape, shape],
        compiler_params=PARAMS,
        name="right_factors",
    )(green_hist)


def put_left(left_high, left_low, p, tile, weight):
    width = tile.shape[-1]
    cols = slice(p * width, (p + 1) * width)
    left_high[:, cols], left_low[:, cols] = split(left_factor(tile, weight))


def contract(left, high_ref, low_ref, first, second):
    high = jnp.concatenate([high_ref[first], high_ref[second]], axis=1)
    low = jnp.concatenate([low_ref[first], low_ref[second]], axis=1)
    return dot3(left, (high, low))


def owner_kernel(
    start_ref, quad_ref, index_ref, win_ref, base_ref, herm_ref, high_ref, low_ref, keep_ref, send_ref, lh, ll, *, scale
):
    past_rows, orbits, width = win_ref.shape
    half = past_rows // 2
    sec_rows = high_ref.shape[0]
    odd = lax.axis_index("second") % 2
    past = lax.axis_index("past")
    for p in range(past_rows):
        put_left(lh, ll, p, win_ref[p], quad_ref[index_ref[p]])
    left = (lh[...], ll[...])
    for out_ref, side in ((send_ref, 1 - odd), (keep_ref, odd)):
        for g in range(out_ref.shape[0]):
            for t in range(0, half, 2):
                spots = [local_spot(start_ref, g * past_rows + side * half + t + q, sec_rows) for q in range(2)]
                acc = contract(left, high_ref, low_ref, spots[0][0], spots[1][0])
                for q in range(2):
                    value = step_size * scale * minus_i_times(acc[:, q * width : (q + 1) * width], orbits)
                    out_ref[g, t + q] = jnp.where(spots[q][1], value, 0.0)
        herm = split(herm_ref[...])
        for t in range(0, half, 2):
            base = jnp.concatenate([base_ref[side * half + t + q] for q in range(2)], axis=1)
            acc = dot3(herm, split(base))
            for q in range(2):
                cols = slice(q * width, (q + 1) * width)
                out_ref[past, t + q] += base[:, cols] + step_size * minus_i_times(acc[:, cols], orbits)


def owner_part(block_start, quad_table, weight_index, window, base, herm, high, low, past_size, scale):
    past_rows, orbits, width = window.shape
    shape = jax.ShapeDtypeStruct((past_size, past_rows // 2, orbits, width), f32)
    return pl.pallas_call(
        lambda *refs: owner_kernel(*refs, scale=scale),
        in_specs=[SMEM_SPEC] * 3 + [VMEM_SPEC] * 5,
        out_specs=[VMEM_SPEC] * 2,
        out_shape=[shape, shape],
        scratch_shapes=[pltpu.VMEM((2 * orbits, past_rows * width), bf16)] * 2,
        compiler_params=PARAMS,
        name="owner_part",
    )(block_start, quad_table, weight_index, window, base, herm, high, low)


def past_half(past_size):
    return lax.axis_index("past") // (past_size // 2) % 2


def integral_kernel(quad_ref, index_ref, mine_ref, other_ref, high_ref, low_ref, *refs, scale, sides, past_size):
    outs, (lh, ll) = refs[: len(sides)], refs[len(sides) :]
    half, orbits, width = mine_ref.shape
    past_rows = 2 * half
    odd = lax.axis_index("second") % 2
    for p in range(past_rows):
        tile = jnp.where(odd == p // half, mine_ref[p % half], other_ref[p % half])
        put_left(lh, ll, p, tile, quad_ref[index_ref[p]])
    left = (lh[...], ll[...])
    for out_ref, kept in zip(outs, sides):
        count = out_ref.shape[0]
        upper = past_half(past_size)
        first = (upper if kept else 1 - upper) * count
        for s in range(0, count, 2):
            acc = contract(left, high_ref, low_ref, first + s, first + s + 1)
            for q in range(2):
                out_ref[s + q] = scale * minus_i_times(acc[:, q * width : (q + 1) * width], orbits)


def integral(quad_table, weight_index, mine, other, high, low, past_size, sides, scale, name):
    half, orbits, width = mine.shape
    shape = jax.ShapeDtypeStruct((high.shape[0] // 2, orbits, width), f32)
    return pl.pallas_call(
        lambda *refs: integral_kernel(*refs, scale=scale, sides=sides, past_size=past_size),
        in_specs=[SMEM_SPEC] * 2 + [VMEM_SPEC] * 4,
        out_specs=[VMEM_SPEC] * len(sides),
        out_shape=[shape] * len(sides),
        scratch_shapes=[pltpu.VMEM((2 * orbits, 2 * half * width), bf16)] * 2,
        compiler_params=PARAMS,
        name=name,
    )(quad_table, weight_index, mine, other, high, low)


def share_kernel(row_ref, mine_ref, recv_ref, herm_ref, out_base_ref, diff_base_ref):
    share, orbits, width = mine_ref.shape
    first = lax.axis_index("past") * share
    herm = split(herm_ref[...])
    for s in range(0, share, 2):

        def pair(ref, start=0):
            return jnp.concatenate([ref[start + s], ref[start + s + 1]], axis=1)

        def ham(value):
            acc = dot3(herm, split(value))
            return jnp.concatenate(
                [minus_i_times(acc[:, q * width : (q + 1) * width], orbits) for q in range(2)], axis=1
            )

        row = pair(row_ref, first)
        slope = ham(row) + (pair(mine_ref) + pair(recv_ref))
        turned = ham(row + step_size * slope)
        out_base = row + 0.5 * step_size * (slope + turned)
        diff_base = 0.5 * step_size * (turned - slope)
        for q in range(2):
            cols = slice(q * width, (q + 1) * width)
            out_base_ref[s + q] = out_base[:, cols]
            diff_base_ref[s + q] = diff_base[:, cols]


def share_bases(green_row, mine, recv, herm):
    shape = jax.ShapeDtypeStruct(mine.shape, f32)
    return pl.pallas_call(
        share_kernel,
        in_specs=[VMEM_SPEC] * 4,
        out_specs=[VMEM_SPEC] * 2,
        out_shape=[shape, shape],
        compiler_params=PARAMS,
        name="share_bases",
    )(green_row, mine, recv, herm)


def finish_kernel(out_base_ref, diff_base_ref, mine_ref, recv_ref, out_ref, square_ref):
    total = jnp.zeros(out_ref.shape[1:], f32)
    for s in range(out_ref.shape[0]):
        last = mine_ref[s] + recv_ref[s]
        out_ref[s] = out_base_ref[s] + last
        diff = diff_base_ref[s] + last
        total = total + diff * diff
    square_ref[...] = jnp.broadcast_to(jnp.sum(total), square_ref.shape)


def finish(out_base, diff_base, mine, recv, devices):
    return pl.pallas_call(
        finish_kernel,
        in_specs=[VMEM_SPEC] * 4,
        out_specs=[VMEM_SPEC] * 2,
        out_shape=[jax.ShapeDtypeStruct(mine.shape, f32), jax.ShapeDtypeStruct((devices, 128), f32)],
        compiler_params=PARAMS,
        name="finish",
    )(out_base, diff_base, mine, recv)


def exchange(value, axis, mask):
    size = lax.axis_size(axis)
    return lax.ppermute(value, axis, [(i, i ^ mask) for i in range(size)])


def pick(value, index, axis=0):
    return lax.dynamic_index_in_dim(value, index, axis, keepdims=False)


def halve_past(value):
    size = value.shape[0]
    half = size // 2
    upper = lax.axis_index("past") // half % 2
    value = value.reshape((2, half) + value.shape[1:])
    return pick(value, upper), exchange(pick(value, 1 - upper), "past", half)


def scatter_past(value):
    while value.shape[0] > 1:
        own, received = halve_past(value)
        value = own + received
    return value[0]


def share_past(keep, send):
    half = lax.axis_size("past") // 2
    received = exchange(send, "past", half)
    while half > 1:
        keep = (keep + received).reshape((half, keep.shape[0] // half) + keep.shape[1:])
        keep, received = halve_past(keep)
        half //= 2
        keep, received = keep.reshape((-1,) + keep.shape[2:]), received.reshape((-1,) + received.shape[2:])
    return keep, received


def gather_past(value):
    size = lax.axis_size("past")
    index = lax.axis_index("past")
    value = value[None]
    mask = 1
    while mask < size:
        other = exchange(value, "past", mask)
        upper = (index // mask) % 2 == 1
        value = jnp.concatenate([jnp.where(upper, other, value), jnp.where(upper, value, other)], axis=0)
        mask *= 2
    return value


def spread_second(value):
    mask = 2
    while mask < lax.axis_size("second"):
        value = value + exchange(value, "second", mask)
        mask *= 2
    return value


def local(green_row, green_hist, hamiltonian, quad_table, weight_index, block_start):
    past_rows, sec_rows, orbits, width = green_hist.shape
    past_size = lax.axis_size("past")
    second_size = lax.axis_size("second")
    total_past = past_rows * past_size
    scale = 1.0 / math.sqrt(orbits * total_past)

    own_window, row_keep, row_send, herm = prepare(block_start, green_row, hamiltonian, past_rows)
    high, low = right_factors(green_hist)

    owner = block_start[0] // sec_rows
    crossing = (block_start[0] + total_past - 1) // sec_rows > owner
    flips = owner ^ (owner + 1)
    branch = jnp.where(crossing, 1, 0)
    masks = []
    while 2 ** len(masks) < second_size:
        masks.append(2 ** (len(masks) + 1) - 1)
    for mask in masks[:-1]:
        branch = branch + jnp.where(crossing & (flips > mask), 1, 0)
    window = lax.switch(
        branch,
        [lambda w: w] + [lambda w, mask=mask: w + exchange(w, "second", mask) for mask in masks],
        own_window,
    )
    part_keep, part_send = owner_part(
        block_start, quad_table, weight_index, window, own_window, herm, high, low, past_size, scale
    )

    row_mine = spread_second(row_keep + exchange(row_send, "second", 1))
    row_other = exchange(row_mine, "second", 1)

    pred_mine = spread_second(scatter_past(part_keep + exchange(part_send, "second", 1)))
    pred_other = exchange(pred_mine, "second", 1)

    slope_keep, slope_send = integral(
        quad_table, weight_index, row_mine, row_other, high, low, past_size, (True, False), scale, "integral_row"
    )
    out_base, diff_base = share_bases(green_row, *share_past(slope_keep, slope_send), herm)

    final = 0.5 * step_size * scale
    (last_send,) = integral(
        quad_table, weight_index, pred_mine, pred_other, high, low, past_size, (False,), final, "integral_send"
    )
    (last_keep,) = integral(
        quad_table, weight_index, pred_mine, pred_other, high, low, past_size, (True,), final, "integral_keep"
    )
    devices = past_size * second_size
    out_share, squares = finish(out_base, diff_base, *share_past(last_keep, last_send), devices)

    sums = lax.all_to_all(squares, ("past", "second"), 0, 0, tiled=True)
    green_next = gather_past(out_share).reshape(green_row.shape)
    total = jnp.sum(sums[:, :1])
    entry_count = sec_rows * second_size * orbits * width
    change = jnp.sqrt(total / entry_count) / step_size
    return (green_next, change.reshape(1))


def solution(mesh):
    placed = (P("second", None, None), P("past", "second", None, None), P(), P(), P("past"), P())
    return jax.shard_map(
        local, mesh=mesh, in_specs=placed, out_specs=(P("second", None, None), P()), check_vma=False
    )
```

```python
import math

import jax
import jax.numpy as jnp
from jax import lax
from jax.experimental import pallas as pl
from jax.experimental.pallas import tpu as pltpu
from jax.sharding import PartitionSpec as P


coupling = 0.5
step_size = 0.25

f32 = jnp.float32
bf16 = jnp.bfloat16
SMEM_SPEC = pl.BlockSpec(memory_space=pltpu.SMEM)
VMEM_SPEC = pl.BlockSpec(memory_space=pltpu.VMEM)
HBM_SPEC = pl.BlockSpec(memory_space=pltpu.HBM)
PARAMS = pltpu.CompilerParams(vmem_limit_bytes=12 << 20)


def split(value):
    high = value.astype(bf16)
    return high, (value - high.astype(f32)).astype(bf16)


def dot3(left, right):
    def one(a, b):
        return jnp.dot(a, b, preferred_element_type=f32)

    return one(left[0], right[0]) + (one(left[0], right[1]) + one(left[1], right[0]))


def swap_halves(tile):
    return pltpu.roll(tile, tile.shape[-1] // 2, tile.ndim - 1)


def is_real(shape):
    return lax.broadcasted_iota(jnp.int32, shape, len(shape) - 1) < shape[-1] // 2


def self_energy(tile):
    square = tile * tile
    return -coupling * (square + swap_halves(square)) * tile


def minus_i_times(acc, orbits):
    turned = swap_halves(acc[:orbits])
    return acc[orbits:] + jnp.where(is_real(turned.shape), turned, -turned)


def left_factor(tile, weight):
    scaled = weight * self_energy(tile)
    plain = weight * tile
    real = is_real(tile.shape)
    return jnp.concatenate(
        [jnp.where(real, scaled, swap_halves(plain)), jnp.where(real, swap_halves(scaled), plain)], axis=0
    )


def local_spot(start_ref, tile, sec_rows):
    spot = start_ref[0] - lax.axis_index("second") * sec_rows + tile
    return jnp.clip(spot, 0, sec_rows - 1), (spot >= 0) & (spot < sec_rows)


def prepare_kernel(
    start_ref, row_ref, ham_hbm, window_ref, keep_ref, send_ref, herm_ref, raw, ham_ref, sems
):
    count = window_ref.shape[0]
    half = count // 2
    orbits = ham_hbm.shape[0]
    sec_rows = row_ref.shape[0]
    first = lax.axis_index("past") * count
    odd = lax.axis_index("second") % 2
    spots = [local_spot(start_ref, first + p, sec_rows) for p in range(count)]
    copies = [pltpu.make_async_copy(row_ref.at[spots[p][0]], raw.at[p], sems.at[p]) for p in range(count)]
    copies.append(pltpu.make_async_copy(ham_hbm, ham_ref, sems.at[count]))
    for copy in copies:
        copy.start()

    copies[-1].wait()
    real = ham_ref[:, :orbits]
    imag = ham_ref[:, orbits:]
    herm_ref[...] = jnp.concatenate([0.5 * (real + real.T), 0.5 * (imag - imag.T)], axis=0)
    for copy in copies[:-1]:
        copy.wait()
    for p in range(count):
        window_ref[p] = jnp.where(spots[p][1], raw[p], 0.0)
    for p in range(half):
        keep_ref[p] = window_ref[odd * half + p]
        send_ref[p] = window_ref[(1 - odd) * half + p]


def prepare(block_start, green_row, hamiltonian, count):
    orbits = hamiltonian.shape[0]
    tile = green_row.shape[1:]
    half = jax.ShapeDtypeStruct((count // 2,) + tile, f32)
    whole = jax.ShapeDtypeStruct((count,) + tile, f32)
    return pl.pallas_call(
        prepare_kernel,
        in_specs=[SMEM_SPEC, HBM_SPEC, HBM_SPEC],
        out_specs=[VMEM_SPEC] * 4,
        out_shape=[
            whole,
            half,
            half,
            jax.ShapeDtypeStruct((2 * orbits, orbits), f32),
        ],
        scratch_shapes=[
            pltpu.VMEM(whole.shape, f32),
            pltpu.VMEM(hamiltonian.shape, f32),
            pltpu.SemaphoreType.DMA((count + 1,)),
        ],
        compiler_params=PARAMS,
        name="prepare",
    )(block_start, green_row, hamiltonian)


def put_left(left_high, left_low, p, tile, weight):
    width = tile.shape[-1]
    cols = slice(p * width, (p + 1) * width)
    left_high[:, cols], left_low[:, cols] = split(left_factor(tile, weight))


def right_factor(tiles):
    return jnp.concatenate(
        [jnp.concatenate(tiles, axis=1), jnp.concatenate([self_energy(t) for t in tiles], axis=1)], axis=0
    )


def contract(left_high, left_low, hist_ref, first, second):
    past_rows, _, _, width = hist_ref.shape
    acc = None
    for p in range(0, past_rows, 2):
        right = jnp.concatenate(
            [right_factor([hist_ref[p + q, first], hist_ref[p + q, second]]) for q in range(2)], axis=0
        )
        cols = slice(p * width, (p + 2) * width)
        term = dot3((left_high[:, cols], left_low[:, cols]), split(right))
        acc = term if acc is None else acc + term
    return acc


def owner_kernel(
    start_ref, quad_ref, index_ref, win_ref, base_ref, herm_ref, hist_ref, keep_ref, send_ref, lh, ll, *, scale
):
    past_rows, orbits, width = win_ref.shape
    half = past_rows // 2
    sec_rows = hist_ref.shape[1]
    odd = lax.axis_index("second") % 2
    past = lax.axis_index("past")
    for p in range(past_rows):
        put_left(lh, ll, p, win_ref[p], quad_ref[index_ref[p]])
    for out_ref, side in ((send_ref, 1 - odd), (keep_ref, odd)):
        for g in range(out_ref.shape[0]):
            for t in range(0, half, 2):
                spots = [local_spot(start_ref, g * past_rows + side * half + t + q, sec_rows) for q in range(2)]
                acc = contract(lh, ll, hist_ref, spots[0][0], spots[1][0])
                for q in range(2):
                    value = step_size * scale * minus_i_times(acc[:, q * width : (q + 1) * width], orbits)
                    out_ref[g, t + q] = jnp.where(spots[q][1], value, 0.0)
        herm = split(herm_ref[...])
        for t in range(0, half, 2):
            base = jnp.concatenate([base_ref[side * half + t + q] for q in range(2)], axis=1)
            acc = dot3(herm, split(base))
            for q in range(2):
                cols = slice(q * width, (q + 1) * width)
                out_ref[past, t + q] += base[:, cols] + step_size * minus_i_times(acc[:, cols], orbits)


def owner_part(block_start, quad_table, weight_index, window, base, herm, green_hist, past_size, scale):
    past_rows, orbits, width = window.shape
    shape = jax.ShapeDtypeStruct((past_size, past_rows // 2, orbits, width), f32)
    return pl.pallas_call(
        lambda *refs: owner_kernel(*refs, scale=scale),
        in_specs=[SMEM_SPEC] * 3 + [VMEM_SPEC] * 4,
        out_specs=[VMEM_SPEC] * 2,
        out_shape=[shape, shape],
        scratch_shapes=[pltpu.VMEM((2 * orbits, past_rows * width), bf16)] * 2,
        compiler_params=PARAMS,
        name="owner_part",
    )(block_start, quad_table, weight_index, window, base, herm, green_hist)


def past_half(past_size):
    return lax.axis_index("past") // (past_size // 2) % 2


def integral_kernel(quad_ref, index_ref, mine_ref, other_ref, hist_ref, *refs, scale, sides, past_size):
    outs, (lh, ll) = refs[: len(sides)], refs[len(sides) :]
    half, orbits, width = mine_ref.shape
    past_rows = 2 * half
    odd = lax.axis_index("second") % 2
    for p in range(past_rows):
        tile = jnp.where(odd == p // half, mine_ref[p % half], other_ref[p % half])
        put_left(lh, ll, p, tile, quad_ref[index_ref[p]])
    for out_ref, kept in zip(outs, sides):
        count = out_ref.shape[0]
        upper = past_half(past_size)
        first = (upper if kept else 1 - upper) * count
        for s in range(0, count, 2):
            acc = contract(lh, ll, hist_ref, first + s, first + s + 1)
            for q in range(2):
                out_ref[s + q] = scale * minus_i_times(acc[:, q * width : (q + 1) * width], orbits)


def integral(quad_table, weight_index, mine, other, green_hist, past_size, sides, scale):
    half, orbits, width = mine.shape
    shape = jax.ShapeDtypeStruct((green_hist.shape[1] // 2, orbits, width), f32)
    return pl.pallas_call(
        lambda *refs: integral_kernel(*refs, scale=scale, sides=sides, past_size=past_size),
        in_specs=[SMEM_SPEC] * 2 + [VMEM_SPEC] * 3,
        out_specs=[VMEM_SPEC] * len(sides),
        out_shape=[shape] * len(sides),
        scratch_shapes=[pltpu.VMEM((2 * orbits, 2 * half * width), bf16)] * 2,
        compiler_params=PARAMS,
    )(quad_table, weight_index, mine, other, green_hist)


def share_kernel(row_ref, mine_ref, recv_ref, herm_ref, out_base_ref, diff_base_ref):
    share, orbits, width = mine_ref.shape
    first = lax.axis_index("past") * share
    herm = split(herm_ref[...])
    for s in range(0, share, 2):

        def pair(ref, start=0):
            return jnp.concatenate([ref[start + s], ref[start + s + 1]], axis=1)

        def ham(value):
            acc = dot3(herm, split(value))
            return jnp.concatenate(
                [minus_i_times(acc[:, q * width : (q + 1) * width], orbits) for q in range(2)], axis=1
            )

        row = pair(row_ref, first)
        slope = ham(row) + (pair(mine_ref) + pair(recv_ref))
        turned = ham(row + step_size * slope)
        out_base = row + 0.5 * step_size * (slope + turned)
        diff_base = 0.5 * step_size * (turned - slope)
        for q in range(2):
            cols = slice(q * width, (q + 1) * width)
            out_base_ref[s + q] = out_base[:, cols]
            diff_base_ref[s + q] = diff_base[:, cols]


def share_bases(green_row, mine, recv, herm):
    shape = jax.ShapeDtypeStruct(mine.shape, f32)
    return pl.pallas_call(
        share_kernel,
        in_specs=[VMEM_SPEC] * 4,
        out_specs=[VMEM_SPEC] * 2,
        out_shape=[shape, shape],
        compiler_params=PARAMS,
        name="share_bases",
    )(green_row, mine, recv, herm)


def finish_kernel(out_base_ref, diff_base_ref, mine_ref, recv_ref, out_ref, square_ref):
    total = jnp.zeros(out_ref.shape[1:], f32)
    for s in range(out_ref.shape[0]):
        last = mine_ref[s] + recv_ref[s]
        out_ref[s] = out_base_ref[s] + last
        diff = diff_base_ref[s] + last
        total = total + diff * diff
    square_ref[...] = jnp.broadcast_to(jnp.sum(total), square_ref.shape)


def finish(out_base, diff_base, mine, recv, devices):
    return pl.pallas_call(
        finish_kernel,
        in_specs=[VMEM_SPEC] * 4,
        out_specs=[VMEM_SPEC] * 2,
        out_shape=[jax.ShapeDtypeStruct(mine.shape, f32), jax.ShapeDtypeStruct((devices, 128), f32)],
        compiler_params=PARAMS,
        name="finish",
    )(out_base, diff_base, mine, recv)


def norm_kernel(sums_ref, out_ref, *, entry_count):
    total = jnp.sum(sums_ref[...], axis=0, keepdims=True)
    out_ref[0] = (jnp.sqrt(total / entry_count) / step_size)[0, 0]


def norm(sums, entry_count):
    return pl.pallas_call(
        lambda *refs: norm_kernel(*refs, entry_count=entry_count),
        in_specs=[VMEM_SPEC],
        out_specs=SMEM_SPEC,
        out_shape=jax.ShapeDtypeStruct((1,), f32),
        compiler_params=PARAMS,
        name="norm",
    )(sums)


def join_kernel(own_ref, other_ref, out_ref, sems, *, mask):
    count = own_ref.shape[0]
    upper = lax.axis_index("past") // mask % 2
    copies = [
        pltpu.make_async_copy(own_ref, out_ref.at[pl.ds(upper * count, count)], sems.at[0]),
        pltpu.make_async_copy(other_ref, out_ref.at[pl.ds((1 - upper) * count, count)], sems.at[1]),
    ]
    for copy in copies:
        copy.start()
    for copy in copies:
        copy.wait()


def join(own, other, mask):
    return pl.pallas_call(
        lambda *refs: join_kernel(*refs, mask=mask),
        in_specs=[VMEM_SPEC, VMEM_SPEC],
        out_specs=HBM_SPEC,
        out_shape=jax.ShapeDtypeStruct((2 * own.shape[0],) + own.shape[1:], f32),
        scratch_shapes=[pltpu.SemaphoreType.DMA((2,))],
        compiler_params=PARAMS,
        name="join",
    )(own, other)


def exchange(value, axis, mask):
    size = lax.axis_size(axis)
    return lax.ppermute(value, axis, [(i, i ^ mask) for i in range(size)])


def pick(value, index, axis=0):
    return lax.dynamic_index_in_dim(value, index, axis, keepdims=False)


def halve_past(value):
    size = value.shape[0]
    half = size // 2
    upper = lax.axis_index("past") // half % 2
    value = value.reshape((2, half) + value.shape[1:])
    return pick(value, upper), exchange(pick(value, 1 - upper), "past", half)


def scatter_past(value):
    while value.shape[0] > 1:
        own, received = halve_past(value)
        value = own + received
    return value[0]


def share_past(keep, send):
    half = lax.axis_size("past") // 2
    received = exchange(send, "past", half)
    while half > 1:
        keep = (keep + received).reshape((half, keep.shape[0] // half) + keep.shape[1:])
        keep, received = halve_past(keep)
        half //= 2
        keep, received = keep.reshape((-1,) + keep.shape[2:]), received.reshape((-1,) + received.shape[2:])
    return keep, received


def gather_past(value):
    mask = 1
    while mask < lax.axis_size("past"):
        value = join(value, exchange(value, "past", mask), mask)
        mask *= 2
    return value


def spread_second(value):
    mask = 2
    while mask < lax.axis_size("second"):
        value = value + exchange(value, "second", mask)
        mask *= 2
    return value


def step(green_row, green_hist, hamiltonian, quad_table, weight_index, block_start):
    past_rows, sec_rows, orbits, width = green_hist.shape
    past_size = lax.axis_size("past")
    second_size = lax.axis_size("second")
    total_past = past_rows * past_size
    scale = 1.0 / math.sqrt(orbits * total_past)

    own_window, row_keep, row_send, herm = prepare(block_start, green_row, hamiltonian, past_rows)

    owner = lax.div(block_start[0], sec_rows)
    crossing = lax.div(block_start[0] + total_past - 1, sec_rows) > owner
    flips = owner ^ (owner + 1)
    branch = jnp.where(crossing, 1, 0)
    masks = []
    while 2 ** len(masks) < second_size:
        masks.append(2 ** (len(masks) + 1) - 1)
    for mask in masks[:-1]:
        branch = branch + jnp.where(crossing & (flips > mask), 1, 0)
    window = lax.switch(
        branch,
        [lambda w: w] + [lambda w, mask=mask: w + exchange(w, "second", mask) for mask in masks],
        own_window,
    )
    part_keep, part_send = owner_part(
        block_start, quad_table, weight_index, window, own_window, herm, green_hist, past_size, scale
    )

    row_mine = spread_second(row_keep + exchange(row_send, "second", 1))
    row_other = exchange(row_mine, "second", 1)

    pred_mine = spread_second(scatter_past(part_keep + exchange(part_send, "second", 1)))
    pred_other = exchange(pred_mine, "second", 1)

    slope_keep, slope_send = integral(
        quad_table, weight_index, row_mine, row_other, green_hist, past_size, (True, False), scale
    )
    out_base, diff_base = share_bases(green_row, *share_past(slope_keep, slope_send), herm)

    final = 0.5 * step_size * scale
    (last_send,) = integral(quad_table, weight_index, pred_mine, pred_other, green_hist, past_size, (False,), final)
    (last_keep,) = integral(quad_table, weight_index, pred_mine, pred_other, green_hist, past_size, (True,), final)
    devices = past_size * second_size
    out_share, squares = finish(out_base, diff_base, *share_past(last_keep, last_send), devices)

    sums = lax.all_to_all(squares, ("past", "second"), 0, 0, tiled=True)
    green_next = gather_past(out_share)
    return (green_next, norm(sums, sec_rows * second_size * orbits * width))


def solution(mesh):
    placed = (P("second", None, None), P("past", "second", None, None), P(), P(), P("past"), P())
    return jax.shard_map(step, mesh=mesh, in_specs=placed, out_specs=(P("second", None, None), P()), check_vma=False)
```

```python
import math

import jax
import jax.numpy as jnp
from jax import lax
from jax.experimental import pallas as pl
from jax.experimental.pallas import tpu as pltpu
from jax.sharding import PartitionSpec as P


coupling = 0.5
step_size = 0.25

f32 = jnp.float32
bf16 = jnp.bfloat16
SMEM_SPEC = pl.BlockSpec(memory_space=pltpu.SMEM)
VMEM_SPEC = pl.BlockSpec(memory_space=pltpu.VMEM)
HBM_SPEC = pl.BlockSpec(memory_space=pltpu.HBM)
PARAMS = pltpu.CompilerParams(vmem_limit_bytes=12 << 20)


def split(value):
    high = value.astype(bf16)
    return high, (value - high.astype(f32)).astype(bf16)


def dot3(left, right):
    def one(a, b):
        return jnp.dot(a, b, preferred_element_type=f32)

    return one(left[0], right[0]) + (one(left[0], right[1]) + one(left[1], right[0]))


def swap_halves(tile):
    return pltpu.roll(tile, tile.shape[-1] // 2, tile.ndim - 1)


def is_real(shape):
    return lax.broadcasted_iota(jnp.int32, shape, len(shape) - 1) < shape[-1] // 2


def self_energy(tile):
    square = tile * tile
    return -coupling * (square + swap_halves(square)) * tile


def minus_i_times(acc, orbits):
    turned = swap_halves(acc[:orbits])
    return acc[orbits:] + jnp.where(is_real(turned.shape), turned, -turned)


def left_factor(tile, weight):
    scaled = weight * self_energy(tile)
    plain = weight * tile
    real = is_real(tile.shape)
    return jnp.concatenate(
        [jnp.where(real, scaled, swap_halves(plain)), jnp.where(real, swap_halves(scaled), plain)], axis=0
    )


def in_hbm(value):
    return pltpu.with_memory_space_constraint(value, pltpu.HBM)


def local_spot(start_ref, tile, sec_rows):
    spot = start_ref[0] - lax.axis_index("second") * sec_rows + tile
    return jnp.clip(spot, 0, sec_rows - 1), (spot >= 0) & (spot < sec_rows)


def prepare_kernel(
    start_ref, row_ref, ham_hbm, window_ref, keep_ref, send_ref, herm_ref, raw, ham_ref, sems
):
    count = window_ref.shape[0]
    half = count // 2
    orbits = ham_hbm.shape[0]
    sec_rows = row_ref.shape[0]
    first = lax.axis_index("past") * count
    odd = lax.axis_index("second") % 2
    spots = [local_spot(start_ref, first + p, sec_rows) for p in range(count)]
    copies = [pltpu.make_async_copy(row_ref.at[spots[p][0]], raw.at[p], sems.at[p]) for p in range(count)]
    copies.append(pltpu.make_async_copy(ham_hbm, ham_ref, sems.at[count]))
    for copy in copies:
        copy.start()

    copies[-1].wait()
    real = ham_ref[:, :orbits]
    imag = ham_ref[:, orbits:]
    herm_ref[...] = jnp.concatenate([0.5 * (real + real.T), 0.5 * (imag - imag.T)], axis=0)
    for copy in copies[:-1]:
        copy.wait()
    for p in range(count):
        window_ref[p] = jnp.where(spots[p][1], raw[p], 0.0)
    for p in range(half):
        keep_ref[p] = window_ref[odd * half + p]
        send_ref[p] = window_ref[(1 - odd) * half + p]


def prepare(block_start, green_row, hamiltonian, count):
    orbits = hamiltonian.shape[0]
    tile = green_row.shape[1:]
    half = jax.ShapeDtypeStruct((count // 2,) + tile, f32)
    whole = jax.ShapeDtypeStruct((count,) + tile, f32)
    return pl.pallas_call(
        prepare_kernel,
        in_specs=[SMEM_SPEC, HBM_SPEC, HBM_SPEC],
        out_specs=[VMEM_SPEC] * 4,
        out_shape=[
            whole,
            half,
            half,
            jax.ShapeDtypeStruct((2 * orbits, orbits), f32),
        ],
        scratch_shapes=[
            pltpu.VMEM(whole.shape, f32),
            pltpu.VMEM(hamiltonian.shape, f32),
            pltpu.SemaphoreType.DMA((count + 1,)),
        ],
        compiler_params=PARAMS,
        name="prepare",
    )(block_start, in_hbm(green_row), in_hbm(hamiltonian))


def put_left(left_high, left_low, p, tile, weight):
    width = tile.shape[-1]
    cols = slice(p * width, (p + 1) * width)
    left_high[:, cols], left_low[:, cols] = split(left_factor(tile, weight))


def right_factor(tiles):
    return jnp.concatenate(
        [jnp.concatenate(tiles, axis=1), jnp.concatenate([self_energy(t) for t in tiles], axis=1)], axis=0
    )


def contract(left_high, left_low, hist_ref, first, second):
    past_rows, _, _, width = hist_ref.shape
    acc = None
    for p in range(0, past_rows, 2):
        right = jnp.concatenate(
            [right_factor([hist_ref[p + q, first], hist_ref[p + q, second]]) for q in range(2)], axis=0
        )
        cols = slice(p * width, (p + 2) * width)
        term = dot3((left_high[:, cols], left_low[:, cols]), split(right))
        acc = term if acc is None else acc + term
    return acc


def owner_kernel(
    start_ref, quad_ref, index_ref, win_ref, base_ref, herm_ref, hist_ref, keep_ref, send_ref, lh, ll, *, scale
):
    past_rows, orbits, width = win_ref.shape
    half = past_rows // 2
    sec_rows = hist_ref.shape[1]
    odd = lax.axis_index("second") % 2
    past = lax.axis_index("past")
    for p in range(past_rows):
        put_left(lh, ll, p, win_ref[p], quad_ref[index_ref[p]])
    for out_ref, side in ((send_ref, 1 - odd), (keep_ref, odd)):
        for g in range(out_ref.shape[0]):
            for t in range(0, half, 2):
                spots = [local_spot(start_ref, g * past_rows + side * half + t + q, sec_rows) for q in range(2)]
                acc = contract(lh, ll, hist_ref, spots[0][0], spots[1][0])
                for q in range(2):
                    value = step_size * scale * minus_i_times(acc[:, q * width : (q + 1) * width], orbits)
                    out_ref[g, t + q] = jnp.where(spots[q][1], value, 0.0)
        herm = split(herm_ref[...])
        for t in range(0, half, 2):
            base = jnp.concatenate([base_ref[side * half + t + q] for q in range(2)], axis=1)
            acc = dot3(herm, split(base))
            for q in range(2):
                cols = slice(q * width, (q + 1) * width)
                out_ref[past, t + q] += base[:, cols] + step_size * minus_i_times(acc[:, cols], orbits)


def owner_part(block_start, quad_table, weight_index, window, base, herm, green_hist, past_size, scale):
    past_rows, orbits, width = window.shape
    shape = jax.ShapeDtypeStruct((past_size, past_rows // 2, orbits, width), f32)
    return pl.pallas_call(
        lambda *refs: owner_kernel(*refs, scale=scale),
        in_specs=[SMEM_SPEC] * 3 + [VMEM_SPEC] * 4,
        out_specs=[VMEM_SPEC] * 2,
        out_shape=[shape, shape],
        scratch_shapes=[pltpu.VMEM((2 * orbits, past_rows * width), bf16)] * 2,
        compiler_params=PARAMS,
        name="owner_part",
    )(block_start, quad_table, weight_index, window, base, herm, green_hist)


def past_half(past_size):
    return lax.axis_index("past") // (past_size // 2) % 2


def integral_kernel(quad_ref, index_ref, mine_ref, other_ref, hist_ref, *refs, scale, sides, past_size):
    outs, (lh, ll) = refs[: len(sides)], refs[len(sides) :]
    half, orbits, width = mine_ref.shape
    past_rows = 2 * half
    odd = lax.axis_index("second") % 2
    for p in range(past_rows):
        tile = jnp.where(odd == p // half, mine_ref[p % half], other_ref[p % half])
        put_left(lh, ll, p, tile, quad_ref[index_ref[p]])
    for out_ref, kept in zip(outs, sides):
        count = out_ref.shape[0]
        upper = past_half(past_size)
        first = (upper if kept else 1 - upper) * count
        for s in range(0, count, 2):
            acc = contract(lh, ll, hist_ref, first + s, first + s + 1)
            for q in range(2):
                out_ref[s + q] = scale * minus_i_times(acc[:, q * width : (q + 1) * width], orbits)


def integral(quad_table, weight_index, mine, other, green_hist, past_size, sides, scale):
    half, orbits, width = mine.shape
    shape = jax.ShapeDtypeStruct((green_hist.shape[1] // 2, orbits, width), f32)
    return pl.pallas_call(
        lambda *refs: integral_kernel(*refs, scale=scale, sides=sides, past_size=past_size),
        in_specs=[SMEM_SPEC] * 2 + [VMEM_SPEC] * 3,
        out_specs=[VMEM_SPEC] * len(sides),
        out_shape=[shape] * len(sides),
        scratch_shapes=[pltpu.VMEM((2 * orbits, 2 * half * width), bf16)] * 2,
        compiler_params=PARAMS,
    )(quad_table, weight_index, mine, other, green_hist)


def share_kernel(row_ref, mine_ref, recv_ref, herm_ref, out_base_ref, diff_base_ref):
    share, orbits, width = mine_ref.shape
    first = lax.axis_index("past") * share
    herm = split(herm_ref[...])
    for s in range(0, share, 2):

        def pair(ref, start=0):
            return jnp.concatenate([ref[start + s], ref[start + s + 1]], axis=1)

        def ham(value):
            acc = dot3(herm, split(value))
            return jnp.concatenate(
                [minus_i_times(acc[:, q * width : (q + 1) * width], orbits) for q in range(2)], axis=1
            )

        row = pair(row_ref, first)
        slope = ham(row) + (pair(mine_ref) + pair(recv_ref))
        turned = ham(row + step_size * slope)
        out_base = row + 0.5 * step_size * (slope + turned)
        diff_base = 0.5 * step_size * (turned - slope)
        for q in range(2):
            cols = slice(q * width, (q + 1) * width)
            out_base_ref[s + q] = out_base[:, cols]
            diff_base_ref[s + q] = diff_base[:, cols]


def share_bases(green_row, mine, recv, herm):
    shape = jax.ShapeDtypeStruct(mine.shape, f32)
    return pl.pallas_call(
        share_kernel,
        in_specs=[VMEM_SPEC] * 4,
        out_specs=[VMEM_SPEC] * 2,
        out_shape=[shape, shape],
        compiler_params=PARAMS,
        name="share_bases",
    )(green_row, mine, recv, herm)


def finish_kernel(out_base_ref, diff_base_ref, mine_ref, recv_ref, square_ref, *out_refs):
    total = jnp.zeros(mine_ref.shape[1:], f32)
    for s in range(mine_ref.shape[0]):
        last = mine_ref[s] + recv_ref[s]
        rows = out_refs[0].shape[0]
        out_refs[s // rows][s % rows] = out_base_ref[s] + last
        diff = diff_base_ref[s] + last
        total = total + diff * diff
    square_ref[...] = jnp.broadcast_to(jnp.sum(total), square_ref.shape)


def finish(out_base, diff_base, mine, recv, devices):
    chunks = 2 if mine.shape[0] % 2 == 0 else 1
    chunk = jax.ShapeDtypeStruct((mine.shape[0] // chunks,) + mine.shape[1:], f32)
    return pl.pallas_call(
        finish_kernel,
        in_specs=[VMEM_SPEC] * 4,
        out_specs=[VMEM_SPEC] * (1 + chunks),
        out_shape=[jax.ShapeDtypeStruct((devices, 128), f32)] + [chunk] * chunks,
        compiler_params=PARAMS,
        name="finish",
    )(out_base, diff_base, mine, recv)


def norm_kernel(sums_ref, out_ref, *, entry_count):
    total = jnp.sum(sums_ref[...], axis=0, keepdims=True)
    out_ref[0] = (jnp.sqrt(total / entry_count) / step_size)[0, 0]


def norm(sums, entry_count):
    return pl.pallas_call(
        lambda *refs: norm_kernel(*refs, entry_count=entry_count),
        in_specs=[VMEM_SPEC],
        out_specs=SMEM_SPEC,
        out_shape=jax.ShapeDtypeStruct((1,), f32),
        compiler_params=PARAMS,
        name="norm",
    )(sums)


def join_kernel(*refs, mask, chunks):
    own, other, out_ref, sems = refs[:chunks], refs[chunks : 2 * chunks], refs[-2], refs[-1]
    rows = own[0].shape[0]
    upper = lax.axis_index("past") // mask % 2
    copies = []
    for side, parts in ((upper, own), (1 - upper, other)):
        for i, part in enumerate(parts):
            target = out_ref.at[pl.ds((side * chunks + i) * rows, rows)]
            copies.append(pltpu.make_async_copy(part, target, sems.at[len(copies)]))
    for copy in copies:
        copy.start()
    for copy in copies:
        copy.wait()


def join(own, other, mask):
    chunks = len(own)
    rows = 2 * chunks * own[0].shape[0]
    return pl.pallas_call(
        lambda *refs: join_kernel(*refs, mask=mask, chunks=chunks),
        in_specs=[VMEM_SPEC] * (2 * chunks),
        out_specs=HBM_SPEC,
        out_shape=jax.ShapeDtypeStruct((rows,) + own[0].shape[1:], f32),
        scratch_shapes=[pltpu.SemaphoreType.DMA((2 * chunks,))],
        compiler_params=PARAMS,
        name="join",
    )(*own, *other)


def exchange(value, axis, mask):
    size = lax.axis_size(axis)
    return lax.ppermute(value, axis, [(i, i ^ mask) for i in range(size)])


def pick(value, index, axis=0):
    return lax.dynamic_index_in_dim(value, index, axis, keepdims=False)


def halve_past(value):
    size = value.shape[0]
    half = size // 2
    upper = lax.axis_index("past") // half % 2
    value = value.reshape((2, half) + value.shape[1:])
    return pick(value, upper), exchange(pick(value, 1 - upper), "past", half)


def scatter_past(value):
    while value.shape[0] > 1:
        own, received = halve_past(value)
        value = own + received
    return value[0]


def share_past(keep, send):
    half = lax.axis_size("past") // 2
    received = exchange(send, "past", half)
    while half > 1:
        keep = (keep + received).reshape((half, keep.shape[0] // half) + keep.shape[1:])
        keep, received = halve_past(keep)
        half //= 2
        keep, received = keep.reshape((-1,) + keep.shape[2:]), received.reshape((-1,) + received.shape[2:])
    return keep, received


def gather_past(chunks):
    mask = 1
    while mask < lax.axis_size("past"):
        others = [exchange(c, "past", mask) for c in chunks]
        chunks = [join(chunks, others, mask)]
        mask *= 2
    return chunks[0]


def spread_second(value):
    mask = 2
    while mask < lax.axis_size("second"):
        value = value + exchange(value, "second", mask)
        mask *= 2
    return value


def step(green_row, green_hist, hamiltonian, quad_table, weight_index, block_start):
    past_rows, sec_rows, orbits, width = green_hist.shape
    past_size = lax.axis_size("past")
    second_size = lax.axis_size("second")
    total_past = past_rows * past_size
    scale = 1.0 / math.sqrt(orbits * total_past)

    own_window, row_keep, row_send, herm = prepare(block_start, green_row, hamiltonian, past_rows)

    owner = lax.div(block_start[0], sec_rows)
    crossing = lax.div(block_start[0] + total_past - 1, sec_rows) > owner
    flips = owner ^ (owner + 1)
    branch = jnp.where(crossing, 1, 0)
    masks = []
    while 2 ** len(masks) < second_size:
        masks.append(2 ** (len(masks) + 1) - 1)
    for mask in masks[:-1]:
        branch = branch + jnp.where(crossing & (flips > mask), 1, 0)
    window = lax.switch(
        branch,
        [lambda w: w] + [lambda w, mask=mask: w + exchange(w, "second", mask) for mask in masks],
        own_window,
    )
    part_keep, part_send = owner_part(
        block_start, quad_table, weight_index, window, own_window, herm, green_hist, past_size, scale
    )

    row_mine = spread_second(row_keep + exchange(row_send, "second", 1))
    row_other = exchange(row_mine, "second", 1)

    pred_mine = spread_second(scatter_past(part_keep + exchange(part_send, "second", 1)))
    pred_other = exchange(pred_mine, "second", 1)

    slope_keep, slope_send = integral(
        quad_table, weight_index, row_mine, row_other, green_hist, past_size, (True, False), scale
    )
    out_base, diff_base = share_bases(green_row, *share_past(slope_keep, slope_send), herm)

    final = 0.5 * step_size * scale
    (last_send,) = integral(quad_table, weight_index, pred_mine, pred_other, green_hist, past_size, (False,), final)
    (last_keep,) = integral(quad_table, weight_index, pred_mine, pred_other, green_hist, past_size, (True,), final)
    devices = past_size * second_size
    squares, *out_chunks = finish(out_base, diff_base, *share_past(last_keep, last_send), devices)

    sums = lax.all_to_all(squares, ("past", "second"), 0, 0, tiled=True)
    green_next = gather_past(out_chunks)
    return (green_next, norm(sums, sec_rows * second_size * orbits * width))


def solution(mesh):
    placed = (P("second", None, None), P("past", "second", None, None), P(), P(), P("past"), P())
    return jax.shard_map(step, mesh=mesh, in_specs=placed, out_specs=(P("second", None, None), P()), check_vma=False)
```

```python
import math

import jax
import jax.numpy as jnp
from jax import lax
from jax.experimental import pallas as pl
from jax.experimental.pallas import tpu as pltpu
from jax.sharding import PartitionSpec as P


coupling = 0.5
step_size = 0.25
LATE_PART = 8

f32 = jnp.float32
bf16 = jnp.bfloat16
SMEM_SPEC = pl.BlockSpec(memory_space=pltpu.SMEM)
VMEM_SPEC = pl.BlockSpec(memory_space=pltpu.VMEM)
HBM_SPEC = pl.BlockSpec(memory_space=pltpu.HBM)
PARAMS = pltpu.CompilerParams(vmem_limit_bytes=12 << 20)


def split(value):
    high = value.astype(bf16)
    return high, (value - high.astype(f32)).astype(bf16)


def dot3(left, right):
    def one(a, b):
        return jnp.dot(a, b, preferred_element_type=f32)

    return one(left[0], right[0]) + (one(left[0], right[1]) + one(left[1], right[0]))


def swap_halves(tile):
    return pltpu.roll(tile, tile.shape[-1] // 2, tile.ndim - 1)


def is_real(shape):
    return lax.broadcasted_iota(jnp.int32, shape, len(shape) - 1) < shape[-1] // 2


def self_energy(tile):
    square = tile * tile
    return -coupling * (square + swap_halves(square)) * tile


def minus_i_times(acc, orbits):
    turned = swap_halves(acc[:orbits])
    return acc[orbits:] + jnp.where(is_real(turned.shape), turned, -turned)


def left_factor(tile, weight):
    scaled = weight * self_energy(tile)
    plain = weight * tile
    real = is_real(tile.shape)
    return jnp.concatenate(
        [jnp.where(real, scaled, swap_halves(plain)), jnp.where(real, swap_halves(scaled), plain)], axis=0
    )


def in_hbm(value):
    return pltpu.with_memory_space_constraint(value, pltpu.HBM)


def local_spot(start_ref, tile, sec_rows):
    spot = start_ref[0] - lax.axis_index("second") * sec_rows + tile
    return jnp.clip(spot, 0, sec_rows - 1), (spot >= 0) & (spot < sec_rows)


def prepare_kernel(
    start_ref, row_ref, ham_hbm, window_ref, keep_ref, send_ref, herm_ref, raw, ham_ref, sems
):
    count = window_ref.shape[0]
    half = count // 2
    orbits = ham_hbm.shape[0]
    sec_rows = row_ref.shape[0]
    first = lax.axis_index("past") * count
    odd = lax.axis_index("second") % 2
    spots = [local_spot(start_ref, first + p, sec_rows) for p in range(count)]
    copies = [pltpu.make_async_copy(row_ref.at[spots[p][0]], raw.at[p], sems.at[p]) for p in range(count)]
    copies.append(pltpu.make_async_copy(ham_hbm, ham_ref, sems.at[count]))
    for copy in copies:
        copy.start()

    copies[-1].wait()
    real = ham_ref[:, :orbits]
    imag = ham_ref[:, orbits:]
    herm_ref[...] = jnp.concatenate([0.5 * (real + real.T), 0.5 * (imag - imag.T)], axis=0)
    for copy in copies[:-1]:
        copy.wait()
    for p in range(count):
        window_ref[p] = jnp.where(spots[p][1], raw[p], 0.0)
    for p in range(half):
        keep_ref[p] = window_ref[odd * half + p]
        send_ref[p] = window_ref[(1 - odd) * half + p]


def prepare(block_start, green_row, hamiltonian, count):
    orbits = hamiltonian.shape[0]
    tile = green_row.shape[1:]
    half = jax.ShapeDtypeStruct((count // 2,) + tile, f32)
    whole = jax.ShapeDtypeStruct((count,) + tile, f32)
    return pl.pallas_call(
        prepare_kernel,
        in_specs=[SMEM_SPEC, HBM_SPEC, HBM_SPEC],
        out_specs=[VMEM_SPEC] * 4,
        out_shape=[
            whole,
            half,
            half,
            jax.ShapeDtypeStruct((2 * orbits, orbits), f32),
        ],
        scratch_shapes=[
            pltpu.VMEM(whole.shape, f32),
            pltpu.VMEM(hamiltonian.shape, f32),
            pltpu.SemaphoreType.DMA((count + 1,)),
        ],
        compiler_params=PARAMS,
        name="prepare",
    )(block_start, in_hbm(green_row), in_hbm(hamiltonian))


def put_left(left_high, left_low, p, tile, weight):
    width = tile.shape[-1]
    cols = slice(p * width, (p + 1) * width)
    left_high[:, cols], left_low[:, cols] = split(left_factor(tile, weight))


def right_factor(tiles):
    return jnp.concatenate(
        [jnp.concatenate(tiles, axis=1), jnp.concatenate([self_energy(t) for t in tiles], axis=1)], axis=0
    )


def contract(left_high, left_low, hist_ref, first, second):
    past_rows, _, _, width = hist_ref.shape
    acc = None
    for p in range(0, past_rows, 2):
        right = jnp.concatenate(
            [right_factor([hist_ref[p + q, first], hist_ref[p + q, second]]) for q in range(2)], axis=0
        )
        cols = slice(p * width, (p + 2) * width)
        term = dot3((left_high[:, cols], left_low[:, cols]), split(right))
        acc = term if acc is None else acc + term
    return acc


def owner_kernel(
    start_ref, quad_ref, index_ref, win_ref, base_ref, herm_ref, hist_ref, keep_ref, send_ref, lh, ll, *, scale
):
    past_rows, orbits, width = win_ref.shape
    half = past_rows // 2
    sec_rows = hist_ref.shape[1]
    odd = lax.axis_index("second") % 2
    past = lax.axis_index("past")
    for p in range(past_rows):
        put_left(lh, ll, p, win_ref[p], quad_ref[index_ref[p]])
    for out_ref, side in ((send_ref, 1 - odd), (keep_ref, odd)):
        for g in range(out_ref.shape[0]):
            for t in range(0, half, 2):
                spots = [local_spot(start_ref, g * past_rows + side * half + t + q, sec_rows) for q in range(2)]
                acc = contract(lh, ll, hist_ref, spots[0][0], spots[1][0])
                for q in range(2):
                    value = step_size * scale * minus_i_times(acc[:, q * width : (q + 1) * width], orbits)
                    out_ref[g, t + q] = jnp.where(spots[q][1], value, 0.0)
        herm = split(herm_ref[...])
        for t in range(0, half, 2):
            base = jnp.concatenate([base_ref[side * half + t + q] for q in range(2)], axis=1)
            acc = dot3(herm, split(base))
            for q in range(2):
                cols = slice(q * width, (q + 1) * width)
                out_ref[past, t + q] += base[:, cols] + step_size * minus_i_times(acc[:, cols], orbits)


def owner_part(block_start, quad_table, weight_index, window, base, herm, green_hist, past_size, scale):
    past_rows, orbits, width = window.shape
    shape = jax.ShapeDtypeStruct((past_size, past_rows // 2, orbits, width), f32)
    return pl.pallas_call(
        lambda *refs: owner_kernel(*refs, scale=scale),
        in_specs=[SMEM_SPEC] * 3 + [VMEM_SPEC] * 4,
        out_specs=[VMEM_SPEC] * 2,
        out_shape=[shape, shape],
        scratch_shapes=[pltpu.VMEM((2 * orbits, past_rows * width), bf16)] * 2,
        compiler_params=PARAMS,
        name="owner_part",
    )(block_start, quad_table, weight_index, window, base, herm, green_hist)


def past_half(past_size):
    return lax.axis_index("past") // (past_size // 2) % 2


def integral_kernel(quad_ref, index_ref, mine_ref, other_ref, hist_ref, *refs, scale, sides, past_size):
    outs, (lh, ll) = refs[: len(sides)], refs[len(sides) :]
    half, orbits, width = mine_ref.shape
    past_rows = 2 * half
    odd = lax.axis_index("second") % 2
    for p in range(past_rows):
        tile = jnp.where(odd == p // half, mine_ref[p % half], other_ref[p % half])
        put_left(lh, ll, p, tile, quad_ref[index_ref[p]])
    for out_ref, kept in zip(outs, sides):
        count = out_ref.shape[0]
        upper = past_half(past_size)
        first = (upper if kept else 1 - upper) * count
        for s in range(0, count, 2):
            acc = contract(lh, ll, hist_ref, first + s, first + s + 1)
            for q in range(2):
                out_ref[s + q] = scale * minus_i_times(acc[:, q * width : (q + 1) * width], orbits)


def integral(quad_table, weight_index, mine, other, green_hist, past_size, sides, scale):
    half, orbits, width = mine.shape
    shape = jax.ShapeDtypeStruct((green_hist.shape[1] // 2, orbits, width), f32)
    return pl.pallas_call(
        lambda *refs: integral_kernel(*refs, scale=scale, sides=sides, past_size=past_size),
        in_specs=[SMEM_SPEC] * 2 + [VMEM_SPEC] * 3,
        out_specs=[VMEM_SPEC] * len(sides),
        out_shape=[shape] * len(sides),
        scratch_shapes=[pltpu.VMEM((2 * orbits, 2 * half * width), bf16)] * 2,
        compiler_params=PARAMS,
    )(quad_table, weight_index, mine, other, green_hist)


def share_kernel(row_ref, mine_ref, recv_ref, herm_ref, out_base_ref, diff_base_ref):
    share, orbits, width = mine_ref.shape
    first = lax.axis_index("past") * share
    herm = split(herm_ref[...])
    for s in range(0, share, 2):

        def pair(ref, start=0):
            return jnp.concatenate([ref[start + s], ref[start + s + 1]], axis=1)

        def ham(value):
            acc = dot3(herm, split(value))
            return jnp.concatenate(
                [minus_i_times(acc[:, q * width : (q + 1) * width], orbits) for q in range(2)], axis=1
            )

        row = pair(row_ref, first)
        slope = ham(row) + (pair(mine_ref) + pair(recv_ref))
        turned = ham(row + step_size * slope)
        out_base = row + 0.5 * step_size * (slope + turned)
        diff_base = 0.5 * step_size * (turned - slope)
        for q in range(2):
            cols = slice(q * width, (q + 1) * width)
            out_base_ref[s + q] = out_base[:, cols]
            diff_base_ref[s + q] = diff_base[:, cols]


def share_bases(green_row, mine, recv, herm):
    shape = jax.ShapeDtypeStruct(mine.shape, f32)
    return pl.pallas_call(
        share_kernel,
        in_specs=[VMEM_SPEC] * 4,
        out_specs=[VMEM_SPEC] * 2,
        out_shape=[shape, shape],
        compiler_params=PARAMS,
        name="share_bases",
    )(green_row, mine, recv, herm)


def finish_kernel(out_base_ref, diff_base_ref, mine_ref, recv_ref, square_ref, *out_refs):
    total = jnp.zeros(mine_ref.shape[1:], f32)
    for s in range(mine_ref.shape[0]):
        last = mine_ref[s] + recv_ref[s]
        chunk, first = 0, 0
        while s >= first + out_refs[chunk].shape[0]:
            first += out_refs[chunk].shape[0]
            chunk += 1
        out_refs[chunk][s - first] = out_base_ref[s] + last
        diff = diff_base_ref[s] + last
        total = total + diff * diff
    square_ref[...] = jnp.broadcast_to(jnp.sum(total), square_ref.shape)


def finish(out_base, diff_base, mine, recv, devices):
    late = mine.shape[0] // LATE_PART
    sizes = [mine.shape[0] - late, late] if late else [mine.shape[0]]
    return pl.pallas_call(
        finish_kernel,
        in_specs=[VMEM_SPEC] * 4,
        out_specs=[VMEM_SPEC] * (1 + len(sizes)),
        out_shape=[jax.ShapeDtypeStruct((devices, 128), f32)]
        + [jax.ShapeDtypeStruct((size,) + mine.shape[1:], f32) for size in sizes],
        compiler_params=PARAMS,
        name="finish",
    )(out_base, diff_base, mine, recv)


def norm_kernel(sums_ref, out_ref, *, entry_count):
    total = jnp.sum(sums_ref[...], axis=0, keepdims=True)
    out_ref[0] = (jnp.sqrt(total / entry_count) / step_size)[0, 0]


def norm(sums, entry_count):
    return pl.pallas_call(
        lambda *refs: norm_kernel(*refs, entry_count=entry_count),
        in_specs=[VMEM_SPEC],
        out_specs=SMEM_SPEC,
        out_shape=jax.ShapeDtypeStruct((1,), f32),
        compiler_params=PARAMS,
        name="norm",
    )(sums)


def join_kernel(*refs, mask, chunks):
    own, other, out_ref, sems = refs[:chunks], refs[chunks : 2 * chunks], refs[-2], refs[-1]
    upper = lax.axis_index("past") // mask % 2
    copies = []
    for side, parts in ((upper, own), (1 - upper, other)):
        first = side * (out_ref.shape[0] // 2)
        for part in parts:
            rows = part.shape[0]
            target = out_ref.at[pl.ds(first, rows)]
            first = first + rows
            copies.append(pltpu.make_async_copy(part, target, sems.at[len(copies)]))
    for copy in copies:
        copy.start()
    for copy in copies:
        copy.wait()


def join(own, other, mask):
    chunks = len(own)
    rows = 2 * sum(part.shape[0] for part in own)
    return pl.pallas_call(
        lambda *refs: join_kernel(*refs, mask=mask, chunks=chunks),
        in_specs=[VMEM_SPEC] * (2 * chunks),
        out_specs=HBM_SPEC,
        out_shape=jax.ShapeDtypeStruct((rows,) + own[0].shape[1:], f32),
        scratch_shapes=[pltpu.SemaphoreType.DMA((2 * chunks,))],
        compiler_params=PARAMS,
        name="join",
    )(*own, *other)


def exchange(value, axis, mask):
    size = lax.axis_size(axis)
    return lax.ppermute(value, axis, [(i, i ^ mask) for i in range(size)])


def pick(value, index, axis=0):
    return lax.dynamic_index_in_dim(value, index, axis, keepdims=False)


def halve_past(value):
    size = value.shape[0]
    half = size // 2
    upper = lax.axis_index("past") // half % 2
    value = value.reshape((2, half) + value.shape[1:])
    return pick(value, upper), exchange(pick(value, 1 - upper), "past", half)


def scatter_past(value):
    while value.shape[0] > 1:
        own, received = halve_past(value)
        value = own + received
    return value[0]


def share_past(keep, send):
    half = lax.axis_size("past") // 2
    received = exchange(send, "past", half)
    while half > 1:
        keep = (keep + received).reshape((half, keep.shape[0] // half) + keep.shape[1:])
        keep, received = halve_past(keep)
        half //= 2
        keep, received = keep.reshape((-1,) + keep.shape[2:]), received.reshape((-1,) + received.shape[2:])
    return keep, received


def gather_past(chunks):
    mask = 1
    while mask < lax.axis_size("past"):
        others = [exchange(c, "past", mask) for c in chunks]
        chunks = [join(chunks, others, mask)]
        mask *= 2
    return chunks[0]


def spread_second(value):
    mask = 2
    while mask < lax.axis_size("second"):
        value = value + exchange(value, "second", mask)
        mask *= 2
    return value


def step(green_row, green_hist, hamiltonian, quad_table, weight_index, block_start):
    past_rows, sec_rows, orbits, width = green_hist.shape
    past_size = lax.axis_size("past")
    second_size = lax.axis_size("second")
    total_past = past_rows * past_size
    scale = 1.0 / math.sqrt(orbits * total_past)

    own_window, row_keep, row_send, herm = prepare(block_start, green_row, hamiltonian, past_rows)

    owner = lax.div(block_start[0], sec_rows)
    crossing = lax.div(block_start[0] + total_past - 1, sec_rows) > owner
    flips = owner ^ (owner + 1)
    branch = jnp.where(crossing, 1, 0)
    masks = []
    while 2 ** len(masks) < second_size:
        masks.append(2 ** (len(masks) + 1) - 1)
    for mask in masks[:-1]:
        branch = branch + jnp.where(crossing & (flips > mask), 1, 0)
    window = lax.switch(
        branch,
        [lambda w: w] + [lambda w, mask=mask: w + exchange(w, "second", mask) for mask in masks],
        own_window,
    )
    part_keep, part_send = owner_part(
        block_start, quad_table, weight_index, window, own_window, herm, green_hist, past_size, scale
    )

    row_mine = spread_second(row_keep + exchange(row_send, "second", 1))
    row_other = exchange(row_mine, "second", 1)

    pred_mine = spread_second(scatter_past(part_keep + exchange(part_send, "second", 1)))
    pred_other = exchange(pred_mine, "second", 1)

    def slope_half(kept):
        return integral(quad_table, weight_index, row_mine, row_other, green_hist, past_size, (kept,), scale)[0]

    slope_send = slope_half(False)
    slope_keep = slope_half(True)
    out_base, diff_base = share_bases(green_row, *share_past(slope_keep, slope_send), herm)

    final = 0.5 * step_size * scale
    (last_send,) = integral(quad_table, weight_index, pred_mine, pred_other, green_hist, past_size, (False,), final)
    (last_keep,) = integral(quad_table, weight_index, pred_mine, pred_other, green_hist, past_size, (True,), final)
    devices = past_size * second_size
    squares, *out_chunks = finish(out_base, diff_base, *share_past(last_keep, last_send), devices)

    sums = lax.all_to_all(squares, ("past", "second"), 0, 0, tiled=True)
    green_next = gather_past(out_chunks)
    return (green_next, norm(sums, sec_rows * second_size * orbits * width))


def solution(mesh):
    placed = (P("second", None, None), P("past", "second", None, None), P(), P(), P("past"), P())
    return jax.shard_map(step, mesh=mesh, in_specs=placed, out_specs=(P("second", None, None), P()), check_vma=False)
```

```python
import math

import jax
import jax.numpy as jnp
from jax import lax
from jax.experimental import pallas as pl
from jax.experimental.pallas import tpu as pltpu
from jax.sharding import PartitionSpec as P


coupling = 0.5
step_size = 0.25

f32 = jnp.float32
bf16 = jnp.bfloat16
SMEM_SPEC = pl.BlockSpec(memory_space=pltpu.SMEM)
VMEM_SPEC = pl.BlockSpec(memory_space=pltpu.VMEM)
HBM_SPEC = pl.BlockSpec(memory_space=pltpu.HBM)
PARAMS = pltpu.CompilerParams(vmem_limit_bytes=12 << 20)


def split(value):
    high = value.astype(bf16)
    return high, (value - high.astype(f32)).astype(bf16)


def dot3(left, right):
    def one(a, b):
        return jnp.dot(a, b, preferred_element_type=f32)

    return one(left[0], right[0]) + (one(left[0], right[1]) + one(left[1], right[0]))


def swap_halves(tile):
    return pltpu.roll(tile, tile.shape[-1] // 2, tile.ndim - 1)


def is_real(shape):
    return lax.broadcasted_iota(jnp.int32, shape, len(shape) - 1) < shape[-1] // 2


def self_energy(tile):
    square = tile * tile
    return -coupling * (square + swap_halves(square)) * tile


def minus_i_times(acc, orbits):
    turned = swap_halves(acc[:orbits])
    return acc[orbits:] + jnp.where(is_real(turned.shape), turned, -turned)


def left_factor(tile, weight):
    scaled = weight * self_energy(tile)
    plain = weight * tile
    real = is_real(tile.shape)
    return jnp.concatenate(
        [jnp.where(real, scaled, swap_halves(plain)), jnp.where(real, swap_halves(scaled), plain)], axis=0
    )


def in_hbm(value):
    return pltpu.with_memory_space_constraint(value, pltpu.HBM)


def local_spot(start_ref, tile, sec_rows):
    spot = start_ref[0] - lax.axis_index("second") * sec_rows + tile
    return jnp.clip(spot, 0, sec_rows - 1), (spot >= 0) & (spot < sec_rows)


def prepare_kernel(
    start_ref, row_ref, ham_hbm, window_ref, keep_ref, send_ref, herm_ref, raw, ham_ref, sems
):
    count = window_ref.shape[0]
    half = count // 2
    orbits = ham_hbm.shape[0]
    sec_rows = row_ref.shape[0]
    first = lax.axis_index("past") * count
    odd = lax.axis_index("second") % 2
    spots = [local_spot(start_ref, first + p, sec_rows) for p in range(count)]
    copies = [pltpu.make_async_copy(row_ref.at[spots[p][0]], raw.at[p], sems.at[p]) for p in range(count)]
    copies.append(pltpu.make_async_copy(ham_hbm, ham_ref, sems.at[count]))
    for copy in copies:
        copy.start()

    copies[-1].wait()
    real = ham_ref[:, :orbits]
    imag = ham_ref[:, orbits:]
    herm_ref[...] = jnp.concatenate([0.5 * (real + real.T), 0.5 * (imag - imag.T)], axis=0)
    for copy in copies[:-1]:
        copy.wait()
    for p in range(count):
        window_ref[p] = jnp.where(spots[p][1], raw[p], 0.0)
    for p in range(half):
        keep_ref[p] = window_ref[odd * half + p]
        send_ref[p] = window_ref[(1 - odd) * half + p]


def prepare(block_start, green_row, hamiltonian, count):
    orbits = hamiltonian.shape[0]
    tile = green_row.shape[1:]
    half = jax.ShapeDtypeStruct((count // 2,) + tile, f32)
    whole = jax.ShapeDtypeStruct((count,) + tile, f32)
    return pl.pallas_call(
        prepare_kernel,
        in_specs=[SMEM_SPEC, HBM_SPEC, HBM_SPEC],
        out_specs=[VMEM_SPEC] * 4,
        out_shape=[
            whole,
            half,
            half,
            jax.ShapeDtypeStruct((2 * orbits, orbits), f32),
        ],
        scratch_shapes=[
            pltpu.VMEM(whole.shape, f32),
            pltpu.VMEM(hamiltonian.shape, f32),
            pltpu.SemaphoreType.DMA((count + 1,)),
        ],
        compiler_params=PARAMS,
        name="prepare",
    )(block_start, in_hbm(green_row), in_hbm(hamiltonian))


def put_left(left_high, left_low, p, tile, weight):
    width = tile.shape[-1]
    cols = slice(p * width, (p + 1) * width)
    left_high[:, cols], left_low[:, cols] = split(left_factor(tile, weight))


def right_factor(tiles):
    return jnp.concatenate(
        [jnp.concatenate(tiles, axis=1), jnp.concatenate([self_energy(t) for t in tiles], axis=1)], axis=0
    )


def contract(left_high, left_low, hist_ref, first, second):
    past_rows, _, _, width = hist_ref.shape
    acc = None
    for p in range(0, past_rows, 2):
        right = jnp.concatenate(
            [right_factor([hist_ref[p + q, first], hist_ref[p + q, second]]) for q in range(2)], axis=0
        )
        cols = slice(p * width, (p + 2) * width)
        term = dot3((left_high[:, cols], left_low[:, cols]), split(right))
        acc = term if acc is None else acc + term
    return acc


def owner_kernel(
    start_ref, quad_ref, index_ref, win_ref, base_ref, herm_ref, hist_ref, keep_ref, send_ref, lh, ll, *, scale
):
    past_rows, orbits, width = win_ref.shape
    half = past_rows // 2
    sec_rows = hist_ref.shape[1]
    odd = lax.axis_index("second") % 2
    past = lax.axis_index("past")
    for p in range(past_rows):
        put_left(lh, ll, p, win_ref[p], quad_ref[index_ref[p]])
    for out_ref, side in ((send_ref, 1 - odd), (keep_ref, odd)):
        for g in range(out_ref.shape[0]):
            for t in range(0, half, 2):
                spots = [local_spot(start_ref, g * past_rows + side * half + t + q, sec_rows) for q in range(2)]
                acc = contract(lh, ll, hist_ref, spots[0][0], spots[1][0])
                for q in range(2):
                    value = step_size * scale * minus_i_times(acc[:, q * width : (q + 1) * width], orbits)
                    out_ref[g, t + q] = jnp.where(spots[q][1], value, 0.0)
        herm = split(herm_ref[...])
        for t in range(0, half, 2):
            base = jnp.concatenate([base_ref[side * half + t + q] for q in range(2)], axis=1)
            acc = dot3(herm, split(base))
            for q in range(2):
                cols = slice(q * width, (q + 1) * width)
                out_ref[past, t + q] += base[:, cols] + step_size * minus_i_times(acc[:, cols], orbits)


def owner_part(block_start, quad_table, weight_index, window, base, herm, green_hist, past_size, scale):
    past_rows, orbits, width = window.shape
    shape = jax.ShapeDtypeStruct((past_size, past_rows // 2, orbits, width), f32)
    return pl.pallas_call(
        lambda *refs: owner_kernel(*refs, scale=scale),
        in_specs=[SMEM_SPEC] * 3 + [VMEM_SPEC] * 4,
        out_specs=[VMEM_SPEC] * 2,
        out_shape=[shape, shape],
        scratch_shapes=[pltpu.VMEM((2 * orbits, past_rows * width), bf16)] * 2,
        compiler_params=PARAMS,
        name="owner_part",
    )(block_start, quad_table, weight_index, window, base, herm, green_hist)


def past_half(past_size):
    return lax.axis_index("past") // (past_size // 2) % 2


def integral_kernel(quad_ref, index_ref, mine_ref, other_ref, hist_ref, *refs, scale, kept, past_size):
    outs, (lh, ll) = refs[:-2], refs[-2:]
    half, orbits, width = mine_ref.shape
    past_rows = 2 * half
    odd = lax.axis_index("second") % 2
    for p in range(past_rows):
        tile = jnp.where(odd == p // half, mine_ref[p % half], other_ref[p % half])
        put_left(lh, ll, p, tile, quad_ref[index_ref[p]])
    upper = past_half(past_size)
    first = (upper if kept else 1 - upper) * sum(out_ref.shape[0] for out_ref in outs)
    for out_ref in outs:
        count = out_ref.shape[0]
        for s in range(0, count, 2):
            acc = contract(lh, ll, hist_ref, first + s, first + s + 1)
            for q in range(2):
                out_ref[s + q] = scale * minus_i_times(acc[:, q * width : (q + 1) * width], orbits)
        first = first + count


def integral(quad_table, weight_index, mine, other, green_hist, past_size, kept, sizes, scale):
    half, orbits, width = mine.shape
    return pl.pallas_call(
        lambda *refs: integral_kernel(*refs, scale=scale, kept=kept, past_size=past_size),
        in_specs=[SMEM_SPEC] * 2 + [VMEM_SPEC] * 3,
        out_specs=[VMEM_SPEC] * len(sizes),
        out_shape=[jax.ShapeDtypeStruct((size, orbits, width), f32) for size in sizes],
        scratch_shapes=[pltpu.VMEM((2 * orbits, 2 * half * width), bf16)] * 2,
        compiler_params=PARAMS,
    )(quad_table, weight_index, mine, other, green_hist)


def share_kernel(row_ref, mine_ref, recv_ref, herm_ref, out_base_ref, diff_base_ref):
    share, orbits, width = mine_ref.shape
    first = lax.axis_index("past") * share
    herm = split(herm_ref[...])
    for s in range(0, share, 2):

        def pair(ref, start=0):
            return jnp.concatenate([ref[start + s], ref[start + s + 1]], axis=1)

        def ham(value):
            acc = dot3(herm, split(value))
            return jnp.concatenate(
                [minus_i_times(acc[:, q * width : (q + 1) * width], orbits) for q in range(2)], axis=1
            )

        row = pair(row_ref, first)
        slope = ham(row) + (pair(mine_ref) + pair(recv_ref))
        turned = ham(row + step_size * slope)
        out_base = row + 0.5 * step_size * (slope + turned)
        diff_base = 0.5 * step_size * (turned - slope)
        for q in range(2):
            cols = slice(q * width, (q + 1) * width)
            out_base_ref[s + q] = out_base[:, cols]
            diff_base_ref[s + q] = diff_base[:, cols]


def share_bases(green_row, mine, recv, herm):
    shape = jax.ShapeDtypeStruct(mine.shape, f32)
    return pl.pallas_call(
        share_kernel,
        in_specs=[VMEM_SPEC] * 4,
        out_specs=[VMEM_SPEC] * 2,
        out_shape=[shape, shape],
        compiler_params=PARAMS,
        name="share_bases",
    )(green_row, mine, recv, herm)


def finish_kernel(*refs, first, last):
    out_base_ref, diff_base_ref, mine_ref, recv_ref = refs[:4]
    out_ref, total_ref = refs[-2:]
    total = refs[4][...] if first else jnp.zeros(out_ref.shape[1:], f32)
    for s in range(out_ref.shape[0]):
        part = mine_ref[first + s] + recv_ref[s]
        out_ref[s] = out_base_ref[first + s] + part
        diff = diff_base_ref[first + s] + part
        total = total + diff * diff
    total_ref[...] = jnp.broadcast_to(jnp.sum(total), total_ref.shape) if last else total


def finish(out_base, diff_base, mine, received, devices):
    first, outs, totals = 0, [], []
    for i, recv in enumerate(received):
        last = i == len(received) - 1
        total_shape = (devices, mine.shape[-1]) if last else mine.shape[1:]
        out, *totals = pl.pallas_call(
            lambda *refs, first=first, last=last: finish_kernel(*refs, first=first, last=last),
            in_specs=[VMEM_SPEC] * (4 + len(totals)),
            out_specs=[VMEM_SPEC] * 2,
            out_shape=[jax.ShapeDtypeStruct(recv.shape, f32), jax.ShapeDtypeStruct(total_shape, f32)],
            compiler_params=PARAMS,
        )(out_base, diff_base, mine, recv, *totals)
        outs.append(out)
        first += recv.shape[0]
    return totals[0], outs


def norm_kernel(sums_ref, out_ref, *, entry_count):
    total = jnp.sum(sums_ref[...], axis=0, keepdims=True)
    out_ref[0] = (jnp.sqrt(total / entry_count) / step_size)[0, 0]


def norm(sums, entry_count):
    return pl.pallas_call(
        lambda *refs: norm_kernel(*refs, entry_count=entry_count),
        in_specs=[VMEM_SPEC],
        out_specs=SMEM_SPEC,
        out_shape=jax.ShapeDtypeStruct((1,), f32),
        compiler_params=PARAMS,
        name="norm",
    )(sums)


def join_kernel(*refs, mask, chunks):
    own, other, out_ref, sems = refs[:chunks], refs[chunks : 2 * chunks], refs[-2], refs[-1]
    upper = lax.axis_index("past") // mask % 2
    copies = []
    for side, parts in ((upper, own), (1 - upper, other)):
        first = side * (out_ref.shape[0] // 2)
        for part in parts:
            rows = part.shape[0]
            target = out_ref.at[pl.ds(first, rows)]
            first = first + rows
            copies.append(pltpu.make_async_copy(part, target, sems.at[len(copies)]))
    for copy in copies:
        copy.start()
    for copy in copies:
        copy.wait()


def join(own, other, mask):
    chunks = len(own)
    rows = 2 * sum(part.shape[0] for part in own)
    return pl.pallas_call(
        lambda *refs: join_kernel(*refs, mask=mask, chunks=chunks),
        in_specs=[VMEM_SPEC] * (2 * chunks),
        out_specs=HBM_SPEC,
        out_shape=jax.ShapeDtypeStruct((rows,) + own[0].shape[1:], f32),
        scratch_shapes=[pltpu.SemaphoreType.DMA((2 * chunks,))],
        compiler_params=PARAMS,
        name="join",
    )(*own, *other)


def exchange(value, axis, mask):
    size = lax.axis_size(axis)
    return lax.ppermute(value, axis, [(i, i ^ mask) for i in range(size)])


def pick(value, index, axis=0):
    return lax.dynamic_index_in_dim(value, index, axis, keepdims=False)


def halve_past(value):
    size = value.shape[0]
    half = size // 2
    upper = lax.axis_index("past") // half % 2
    value = value.reshape((2, half) + value.shape[1:])
    return pick(value, upper), exchange(pick(value, 1 - upper), "past", half)


def scatter_past(value):
    while value.shape[0] > 1:
        own, received = halve_past(value)
        value = own + received
    return value[0]


def share_past(keep, send):
    half = lax.axis_size("past") // 2
    received = exchange(send, "past", half)
    while half > 1:
        keep = (keep + received).reshape((half, keep.shape[0] // half) + keep.shape[1:])
        keep, received = halve_past(keep)
        half //= 2
        keep, received = keep.reshape((-1,) + keep.shape[2:]), received.reshape((-1,) + received.shape[2:])
    return keep, received


def gather_past(chunks):
    mask = 1
    while mask < lax.axis_size("past"):
        others = [exchange(c, "past", mask) for c in chunks]
        chunks = [join(chunks, others, mask)]
        mask *= 2
    return chunks[0]


def spread_second(value):
    mask = 2
    while mask < lax.axis_size("second"):
        value = value + exchange(value, "second", mask)
        mask *= 2
    return value


def step(green_row, green_hist, hamiltonian, quad_table, weight_index, block_start):
    past_rows, sec_rows, orbits, width = green_hist.shape
    past_size = lax.axis_size("past")
    second_size = lax.axis_size("second")
    total_past = past_rows * past_size
    scale = 1.0 / math.sqrt(orbits * total_past)

    own_window, row_keep, row_send, herm = prepare(block_start, green_row, hamiltonian, past_rows)

    owner = lax.div(block_start[0], sec_rows)
    crossing = lax.div(block_start[0] + total_past - 1, sec_rows) > owner
    flips = owner ^ (owner + 1)
    branch = jnp.where(crossing, 1, 0)
    masks = []
    while 2 ** len(masks) < second_size:
        masks.append(2 ** (len(masks) + 1) - 1)
    for mask in masks[:-1]:
        branch = branch + jnp.where(crossing & (flips > mask), 1, 0)
    window = lax.switch(
        branch,
        [lambda w: w] + [lambda w, mask=mask: w + exchange(w, "second", mask) for mask in masks],
        own_window,
    )
    part_keep, part_send = owner_part(
        block_start, quad_table, weight_index, window, own_window, herm, green_hist, past_size, scale
    )

    row_mine = spread_second(row_keep + exchange(row_send, "second", 1))
    row_other = exchange(row_mine, "second", 1)

    pred_mine = spread_second(scatter_past(part_keep + exchange(part_send, "second", 1)))
    pred_other = exchange(pred_mine, "second", 1)

    def slope_half(kept):
        return integral(
            quad_table, weight_index, row_mine, row_other, green_hist, past_size, kept, [sec_rows // 2], scale
        )[0]

    slope_send = slope_half(False)
    slope_keep = slope_half(True)
    out_base, diff_base = share_bases(green_row, *share_past(slope_keep, slope_send), herm)

    final = 0.5 * step_size * scale
    share_rows = sec_rows // past_size
    late = share_rows // 8 * 2 if past_size == 2 else 0
    sizes = [sec_rows // 2 - late, late] if late else [sec_rows // 2]

    def last_half(kept, sizes):
        return integral(quad_table, weight_index, pred_mine, pred_other, green_hist, past_size, kept, sizes, final)

    last_send = last_half(False, sizes)
    (last_keep,) = last_half(True, [sec_rows // 2])
    if late:
        last_recv = [exchange(c, "past", 1) for c in last_send]
    else:
        last_keep, received = share_past(last_keep, last_send[0])
        last_recv = [received]
    squares, out_chunks = finish(out_base, diff_base, last_keep, last_recv, past_size * second_size)

    sums = lax.all_to_all(squares, ("past", "second"), 0, 0, tiled=True)
    green_next = gather_past(out_chunks)
    return (green_next, norm(sums, sec_rows * second_size * orbits * width))


def solution(mesh):
    placed = (P("second", None, None), P("past", "second", None, None), P(), P(), P("past"), P())
    return jax.shard_map(step, mesh=mesh, in_specs=placed, out_specs=(P("second", None, None), P()), check_vma=False)
```
